32 devices in a mesh: dp: 32 (over z, y, x, core).
Axes of the slice: x: 2, y: 2, z: 4, core: 2. Of those that a mesh axis runs over, the one named last changes fastest.
Arguments:
- tokens: bfloat16 [8192, 2048], P('dp'), may hold values from -6 to 6
- cotangent: bfloat16 [8192, 2048], P('dp'), may hold values from -6 to 6
- send_row: int32 [8192], P('dp'), may hold values from 0 to 256, as said below
- recv_slot: int32 [4096], P('dp'), may hold values from 0 to 255, as said below
- segment: int32 [4096], P('dp'), may hold values from 0 to 1, as said below
- query_weight: bfloat16 [2048, 2048], P('dp'), may hold values from -0.125 to 0.125
- key_projection_weight: bfloat16 [2048, 512], P('dp'), may hold values from -0.125 to 0.125
- value_projection_weight: bfloat16 [2048, 512], P('dp'), may hold values from -0.125 to 0.125
- out_weight: bfloat16 [2048, 2048], P('dp'), may hold values from -1 to 1
- attn_gain: bfloat16 [2048], P('dp'), may hold values from 0.5 to 1.5
- gate_weight: bfloat16 [2048, 5632], P('dp'), may hold values from -0.125 to 0.125
- up_weight: bfloat16 [2048, 5632], P('dp'), may hold values from -0.125 to 0.125
- down_weight: bfloat16 [5632, 2048], P('dp'), may hold values from -0.078125 to 0.078125
- ffn_gain: bfloat16 [2048], P('dp'), may hold values from 0.5 to 1.5
Outputs:
- output: bfloat16 [8192, 2048], P('dp')
- input_grad: bfloat16 [8192, 2048], P('dp')
- query_grad: float32 [2048, 2048], P('dp')
- key_grad: float32 [2048, 512], P('dp')
- value_grad: float32 [2048, 512], P('dp')
- out_grad: float32 [2048, 2048], P('dp')
- attn_gain_grad: float32 [2048], P('dp')
- gate_grad: float32 [2048, 5632], P('dp')
- up_grad: float32 [2048, 5632], P('dp')
- down_grad: float32 [5632, 2048], P('dp')
- ffn_gain_grad: float32 [2048], P('dp')
The draws below stay inside these ranges and needn't reach their ends.
Inputs may be any that keep to these rules, and one draw needn't show every extreme that they name: `send_row`: slots e * 8 to e * 8 + 7 of a device's block hold, first to last, the local rows it sends to device e; a peer's rows fill the first slots of its part and the others hold 256. Every device sends exactly 128 of its rows, each at most once, and sends 8 rows to some peer; a row that is sent nowhere belongs to a sample that skips the layer. `recv_slot`: the work rows of device e list every arrival slot p * 8 + j of device e that holds a row (j below what device p sends to e) exactly once; each device works on exactly 128 rows, and receives 8 rows from some peer. `segment`: on each device the sample numbers start at 0, never fall, and rise only at work rows whose index is a multiple of 64, so a sample's rows are consecutive work rows of one device; some device works on a single sample of 128 rows, and some other device starts a new sample at every multiple of 64.
All inputs are finite; a program needn't handle non-finite values.
Results may differ from the reference program's by a relative error of at most 0.014.
Values may be sent and summed in bfloat16 or wider, within the bound.
No kernel may reach another device: no remote copies, remote signals or barrier semaphores. Data moves between devices by JAX's collectives and lax.ppermute only.
A program may use at most 384 MiB of HBM per device.

```python
from functools import partial
import jax
import jax.numpy as jnp
from jax import lax

MODEL_DIM = 2048
QUERY_HEADS = 16
KEY_VALUE_HEADS = 4
HEAD_DIM = 128
FF = 5632
WORK = 128
SAMPLE_MIN = 64
TOK_DEV = 256
CAP = 8
TOKENS = 8192
N_DP = 32


def routing(key):
    peer_total = N_DP
    keys_all = jax.random.split(jax.random.fold_in(key, 11), 8)
    half_cap = CAP // 2
    shifts = jax.random.randint(keys_all[0], (peer_total // 2,), -half_cap, half_cap + 1)
    shifts = shifts.at[0].set(half_cap)
    loads = jnp.stack([half_cap + shifts, half_cap - shifts], axis=1).reshape(peer_total)
    loads = loads[jax.random.permutation(keys_all[1], peer_total)]
    row_perm = jax.random.permutation(keys_all[2], peer_total)
    col_perm = jax.random.permutation(keys_all[3], peer_total)
    counts = loads[(col_perm[None, :] - row_perm[:, None]) % peer_total]
    slot_count = peer_total * CAP
    slot_index = jnp.arange(slot_count, dtype=jnp.int32)
    slot_peer = slot_index // CAP
    slot_lane = slot_index % CAP
    sent = slot_lane[None, :] < counts[:, slot_peer]
    rank_sent = jnp.cumsum(sent.astype(jnp.int32), axis=1) - 1
    local_perm = jax.vmap(partial(jax.random.permutation, x=TOK_DEV))(jax.random.split(keys_all[4], peer_total))
    picked = jnp.take_along_axis(local_perm, jnp.maximum(rank_sent, 0), axis=1)
    send_table = jnp.where(sent, picked, TOK_DEV).astype(jnp.int32)
    arrived = slot_lane[None, :] < counts[slot_peer, :].T
    order_rand = jax.vmap(partial(jax.random.permutation, x=slot_count))(jax.random.split(keys_all[5], peer_total))
    sort_key = jnp.where(arrived, 0, slot_count) + order_rand
    recv_table = jnp.argsort(sort_key, axis=1, stable=True)[:, :WORK].astype(jnp.int32)
    work_index = jnp.arange(WORK, dtype=jnp.int32)
    grid_cut = (work_index % SAMPLE_MIN == 0) & (work_index > 0)
    coin = jax.random.randint(keys_all[6], (peer_total, WORK), 0, 2) == 0
    cuts = grid_cut[None, :] & coin
    single = jax.random.randint(keys_all[7], (), 0, peer_total)
    busiest = (single + 1) % peer_total
    device_index = jnp.arange(peer_total, dtype=jnp.int32)[:, None]
    cuts = jnp.where(device_index == busiest, grid_cut[None, :], cuts)
    cuts = jnp.where(device_index == single, False, cuts)
    seg_table = jnp.cumsum(cuts.astype(jnp.int32), axis=1).astype(jnp.int32)
    return (send_table.reshape(-1), recv_table.reshape(-1), seg_table.reshape(-1))


def draw_send_row(key, part):
    return routing(key)[0]


def draw_recv_slot(key, part):
    return routing(key)[1]


def draw_segment(key, part):
    return routing(key)[2]


def block_levels(rng, dims, pieces, least, largest):
    factor_of = 1.0
    for axis_at, shards_of in pieces:
        steps = jax.random.uniform(jax.random.fold_in(jax.random.fold_in(rng, 6), axis_at), (shards_of,), jnp.float32, least / len(pieces), largest / len(pieces))
        factor_of = factor_of * jnp.repeat(jnp.exp(steps), dims[axis_at] // shards_of).reshape((-1,) + (1,) * (len(dims) - 1 - axis_at))
    return factor_of


def gaussian(rng, shape, scale, limit, shards=(), kind=jnp.bfloat16):
    level = block_levels(rng, shape, shards, -0.22, 0.18) if shards else 1.0
    values = jax.random.normal(rng, shape, jnp.float32) * scale * level
    return jnp.minimum(jnp.maximum(values, -limit), limit).astype(kind)


def setup_inputs(seed: int = 0) -> dict:
    splits = jax.random.split(jax.random.key(seed), 15)
    return {
        "tokens": gaussian(splits[0], (TOKENS, MODEL_DIM), 1.0, 6.0, ((0, 32),)),
        "cotangent": gaussian(splits[1], (TOKENS, MODEL_DIM), 1.0, 6.0, ((0, 32),)),
        "send_row": draw_send_row(jax.random.fold_in(splits[14], 71), 0),
        "recv_slot": draw_recv_slot(jax.random.fold_in(splits[14], 71), 0),
        "segment": draw_segment(jax.random.fold_in(splits[14], 71), 0),
        "query_weight": gaussian(splits[5], (MODEL_DIM, QUERY_HEADS * HEAD_DIM), MODEL_DIM ** -0.5, 0.125, ((0, 32),)),
        "key_projection_weight": gaussian(splits[6], (MODEL_DIM, KEY_VALUE_HEADS * HEAD_DIM), MODEL_DIM ** -0.5, 0.125, ((0, 32),)),
        "value_projection_weight": gaussian(splits[7], (MODEL_DIM, KEY_VALUE_HEADS * HEAD_DIM), MODEL_DIM ** -0.5, 0.125, ((0, 32),)),
        "out_weight": gaussian(splits[8], (QUERY_HEADS * HEAD_DIM, MODEL_DIM), (QUERY_HEADS * HEAD_DIM // 64) ** -0.5, 1.0, ((0, 32),)),
        "attn_gain": jnp.clip(1.0 + 0.1 * jax.random.normal(splits[9], (MODEL_DIM,), jnp.float32), 0.5, 1.5).astype(jnp.bfloat16),
        "gate_weight": gaussian(splits[10], (MODEL_DIM, FF), MODEL_DIM ** -0.5, 0.125, ((0, 32),)),
        "up_weight": gaussian(splits[11], (MODEL_DIM, FF), MODEL_DIM ** -0.5, 0.125, ((0, 32),)),
        "down_weight": gaussian(splits[12], (FF, MODEL_DIM), FF ** -0.5, 0.078125, ((0, 32),)),
        "ffn_gain": jnp.clip(1.0 + 0.1 * jax.random.normal(splits[13], (MODEL_DIM,), jnp.float32), 0.5, 1.5).astype(jnp.bfloat16),
    }


@jax.custom_vjp
def lower_precision(v):
    return lax.optimization_barrier(v.astype(jnp.bfloat16)).astype(jnp.float32)

@jax.custom_vjp
def lower_precision_backward(v):
    return v

def low_keep(v):
    return (lower_precision(v), None)

def low_pass(kept, grad):
    return (grad,)

def back_keep(v):
    return (v, None)

def back_low(kept, grad):
    return (lower_precision(grad),)
lower_precision.defvjp(low_keep, low_pass)
lower_precision_backward.defvjp(back_keep, back_low)
epsilon = 1e-05
rope_base = 10000.0
highest = lax.Precision.HIGHEST

def matrix_multiply(left, right):
    return jnp.dot(left, right, precision=highest, preferred_element_type=jnp.float32)

def angles(position, head_width):
    freq = rope_base ** (-(jnp.arange(head_width // 2, dtype=jnp.float32) * 2.0) / head_width)
    phase = position.astype(jnp.float32)[:, None] * freq[None, :]
    phase = jnp.concatenate([phase, phase], axis=1)
    return (jnp.cos(phase), jnp.sin(phase))

def positions(segment_ids):
    row_index = jnp.arange(segment_ids.shape[0], dtype=jnp.int32)
    seg_first = jnp.concatenate([jnp.ones((1,), dtype=bool), segment_ids[1:] != segment_ids[:-1]])
    seg_start = lax.cummax(jnp.where(seg_first, row_index, 0), axis=0)
    return row_index - seg_start

def rotary_heads(values_in, cosine_table, sine_lookup):
    half_width = values_in.shape[-1] // 2
    turned = jnp.concatenate([-values_in[..., half_width:], values_in[..., :half_width]], axis=-1)
    return values_in * cosine_table[:, None, :] + turned * sine_lookup[:, None, :]

def block_rows(work_rows, segment_ids, params):
    query_w, key_matrix, value_matrix, out_w, gain_one, gate_w, up_w, down_w, gain_two = params
    total_row_count = work_rows.shape[0]
    work_rows = lower_precision_backward(work_rows)
    scale_one = lax.rsqrt(lax.optimization_barrier(jnp.mean(work_rows * work_rows, axis=-1, keepdims=True)) + epsilon)
    first_normalized = lower_precision(work_rows * scale_one * gain_one)
    cosine_table, sine_lookup = angles(positions(segment_ids), HEAD_DIM)
    query_projection = lower_precision_backward(matrix_multiply(first_normalized, query_w)).reshape(total_row_count, QUERY_HEADS, HEAD_DIM)
    key_projection = lower_precision_backward(matrix_multiply(first_normalized, key_matrix)).reshape(total_row_count, KEY_VALUE_HEADS, HEAD_DIM)
    value_rows = lower_precision(lower_precision_backward(matrix_multiply(first_normalized, value_matrix))).reshape(total_row_count, KEY_VALUE_HEADS, HEAD_DIM)
    rotated_query = lower_precision(rotary_heads(query_projection, cosine_table, sine_lookup)).reshape(total_row_count, KEY_VALUE_HEADS, QUERY_HEADS // KEY_VALUE_HEADS, HEAD_DIM)
    key_rot = lower_precision(rotary_heads(key_projection, cosine_table, sine_lookup))
    row_index = jnp.arange(total_row_count, dtype=jnp.int32)
    allowed = (segment_ids[:, None] == segment_ids[None, :]) & (row_index[None, :] <= row_index[:, None])
    scores = lower_precision_backward(jnp.einsum('qagd,kad->agqk', rotated_query, key_rot, precision=highest) * HEAD_DIM ** (-0.5))
    scores = jnp.where(allowed[None, None], scores, -1e+30)
    row_max = lax.optimization_barrier(jnp.max(scores, axis=-1, keepdims=True))
    exp_scores = jnp.exp(scores - row_max)
    attn_prob = lower_precision(exp_scores / lax.optimization_barrier(jnp.sum(exp_scores, axis=-1, keepdims=True)))
    head_out = jnp.einsum('agqk,kad->qagd', attn_prob, value_rows, precision=highest).reshape(total_row_count, QUERY_HEADS * HEAD_DIM)
    head_out = lower_precision(lower_precision_backward(head_out))
    attn = lower_precision_backward(matrix_multiply(head_out, out_w))
    hidden_one = work_rows + attn
    scale_two = lax.rsqrt(lax.optimization_barrier(jnp.mean(hidden_one * hidden_one, axis=-1, keepdims=True)) + epsilon)
    normed_two = lower_precision(hidden_one * scale_two * gain_two)
    gate_pre = lower_precision_backward(matrix_multiply(normed_two, gate_w))
    up_pre = lower_precision_backward(matrix_multiply(normed_two, up_w))
    act_rows = lower_precision(jax.nn.silu(gate_pre) * up_pre)
    ffn_rows = lower_precision_backward(matrix_multiply(act_rows, down_w))
    return lower_precision(attn + ffn_rows)

def reference(tokens, cotangent, send_row, recv_slot, segment, query_weight, key_projection_weight, value_projection_weight, out_weight, attn_gain, gate_weight, up_weight, down_weight, ffn_gain):
    source_rows = send_row.reshape(N_DP, N_DP * CAP)
    slot_table = recv_slot.reshape(N_DP, WORK)
    peer_index = slot_table // CAP
    lane_index = slot_table % CAP
    dest_index = jnp.arange(N_DP, dtype=jnp.int32)[:, None]
    local_row = source_rows[peer_index, dest_index * CAP + lane_index]
    global_row = (peer_index * TOK_DEV + local_row).reshape(-1).astype(jnp.int32)
    token_f = tokens.astype(jnp.float32)
    cot_f = cotangent.astype(jnp.float32)
    work_in = token_f[global_row].reshape(N_DP, WORK, MODEL_DIM)
    work_cot = cot_f[global_row].reshape(N_DP, WORK, MODEL_DIM)
    seg_blocks = segment.reshape(N_DP, WORK)
    params = tuple((weight.astype(jnp.float32) for weight in (query_weight, key_projection_weight, value_projection_weight, out_weight, attn_gain, gate_weight, up_weight, down_weight, ffn_gain)))

    def forward(rows_all, params_all):

        def one_block(block_items):
            return block_rows(block_items[0], block_items[1], params_all)
        return lax.map(jax.checkpoint(one_block), (rows_all, seg_blocks))
    delta, pullback = jax.vjp(forward, work_in, params)
    back_rows, grads = pullback(work_cot)
    zeros_rows = jnp.zeros((TOKENS, MODEL_DIM), dtype=jnp.float32)
    output = (token_f + zeros_rows.at[global_row].set(delta.reshape(-1, MODEL_DIM))).astype(jnp.bfloat16)
    input_grad = (cot_f + zeros_rows.at[global_row].set(back_rows.reshape(-1, MODEL_DIM))).astype(jnp.bfloat16)
    return (output, input_grad, grads[0], grads[1], grads[2], grads[3], grads[4], grads[5], grads[6], grads[7], grads[8])
```

```python
import jax
import jax.numpy as jnp
import numpy as np
from jax import lax
from jax.sharding import Mesh, PartitionSpec as P

QUERY_HEADS = 16
KEY_VALUE_HEADS = 4
HEAD_DIM = 128
GROUP = QUERY_HEADS // KEY_VALUE_HEADS

epsilon = 1e-05
rope_base = 10000.0

ALL = ("h", "l", "y", "x", "c")
T = ("l", "y")
D = ("h", "x", "c")
F32 = jnp.float32
BF16 = jnp.bfloat16


def dot(left, right):
    return jnp.dot(left, right, preferred_element_type=F32)


def dot_tn(left, right):
    return lax.dot_general(left, right, (((0,), (0,)), ((), ())), preferred_element_type=F32)


def dot_nt(left, right):
    return lax.dot_general(left, right, (((1,), (1,)), ((), ())), preferred_element_type=F32)


def gather_t(rows):
    return lax.all_gather(rows, T, axis=0, tiled=True)


def scatter_t(partial):
    return lax.psum_scatter(partial.astype(BF16), T, scatter_dimension=0, tiled=True).astype(F32)


def gather_d(block):
    return lax.all_gather(block, D, axis=0, tiled=False)


def scatter_d(partial):
    return lax.psum_scatter(partial, D, scatter_dimension=0, tiled=True)


def norm_back(grad_out, values_in, scale_rows, gain_row):
    scaled_grad = grad_out * gain_row
    grad_in = scale_rows * scaled_grad - values_in * scale_rows**3 * jnp.mean(
        scaled_grad * values_in, axis=-1, keepdims=True
    )
    grad_gain = jnp.sum(grad_out * values_in * scale_rows, axis=0)
    return (grad_in, grad_gain)


def turn(values_in):
    half = values_in.shape[-1] // 2
    return jnp.concatenate([-values_in[..., half:], values_in[..., :half]], axis=-1)


def turn_back(values_in):
    half = values_in.shape[-1] // 2
    return jnp.concatenate([values_in[..., half:], -values_in[..., :half]], axis=-1)


def make(n):
    nh = n // 16
    nt = 4
    nd = n // nt

    def ff_split(block, ffb):
        rows = block.shape[0]
        b = block.reshape(rows, nh, nt, 4 * ffb)
        return jnp.transpose(b, (2, 0, 1, 3)).reshape(nt, rows, nd * ffb)

    def ff_join(parts, ffb):
        rows = parts.shape[1]
        b = parts.reshape(nt, rows, nh, 4 * ffb)
        return jnp.transpose(b, (1, 2, 0, 3)).reshape(rows, n * ffb)

    def full_rows(mine):
        rows, cols = mine.shape[1:]
        g = gather_d(mine).reshape(nh, 2, 2, 2, 2, rows, cols)
        return jnp.transpose(g, (0, 3, 4, 1, 2, 5, 6)).reshape(n * rows, cols)

    def own_rows(full, rows):
        cols = full.shape[1]
        g = full.reshape(nh, 2, 2, 2, 2, rows, cols)
        g = jnp.transpose(g, (0, 3, 4, 1, 2, 5, 6)).reshape(nd * nt * rows, cols)
        g = scatter_d(g).reshape(nt, rows, cols)
        return lax.all_to_all(g, T, split_axis=0, concat_axis=0, tiled=True)

    head_bits = n // KEY_VALUE_HEADS
    perm = []
    for src in range(n):
        a, rest = divmod(src, head_bits)
        h, xc = divmod(rest, 4)
        perm.append((src, h * 16 + a * 4 + xc))
    unperm = [(b, a) for a, b in perm]

    def shards(
        tokens,
        cotangent,
        send_row,
        recv_slot,
        segment,
        query_weight,
        key_weight,
        value_weight,
        out_weight,
        attn_gain,
        gate_weight,
        up_weight,
        down_weight,
        ffn_gain,
    ):
        width = tokens.shape[1]
        work = recv_slot.shape[0]
        slots = send_row.shape[0]
        cap = slots // n
        gw = attn_gain.shape[0]
        ffb = down_weight.shape[0]
        ff = nd * ffb
        factor = HEAD_DIM ** (-0.5)
        extra = -(-max(2 * gw, work) // 128) * 128

        heads = jnp.concatenate(
            [
                query_weight.reshape(gw, nt, GROUP * HEAD_DIM),
                key_weight.reshape(gw, nt, HEAD_DIM),
                value_weight.reshape(gw, nt, HEAD_DIM),
            ],
            axis=2,
        )
        heads = jnp.transpose(heads, (1, 0, 2))
        heads = lax.all_to_all(heads, T, split_axis=0, concat_axis=0, tiled=True)
        w_qkv = full_rows(heads)
        w_out = gather_d(lax.ppermute(out_weight, ALL, perm)).reshape(-1, width)
        gu = jnp.concatenate([ff_split(gate_weight, ffb), ff_split(up_weight, ffb)], axis=2)
        gu = lax.all_to_all(gu, T, split_axis=0, concat_axis=0, tiled=True)
        w_gu = full_rows(gu)
        w_down = gather_d(down_weight).reshape(ff, width)

        gains = jnp.concatenate([attn_gain, ffn_gain])
        ext = jnp.zeros((cap, extra), BF16)
        ext = ext.at[0, : 2 * gw].set(gains).at[1, :work].set(segment.astype(BF16))
        ext = jnp.broadcast_to(ext[None], (n, cap, extra)).reshape(slots, extra)
        out_rows = jnp.take(tokens, send_row, axis=0, mode="fill", fill_value=0)
        out_rows = jnp.concatenate([out_rows, ext], axis=1)
        out_cots = jnp.take(cotangent, send_row, axis=0, mode="fill", fill_value=0)
        come = lax.all_to_all(out_rows, ALL, split_axis=0, concat_axis=0, tiled=True)
        come_cots = lax.all_to_all(out_cots, ALL, split_axis=0, concat_axis=0, tiled=True)
        rows_bf = jnp.take(come[:, :width], recv_slot, axis=0)
        grad_bf = jnp.take(come_cots, recv_slot, axis=0)
        ext = come[:, width:].reshape(n, cap, extra)
        gain_one = ext[:, 0, :gw].reshape(n * gw).astype(F32)
        gain_two = ext[:, 0, gw : 2 * gw].reshape(n * gw).astype(F32)
        seg = ext[:, 1, :work].reshape(nh, nt, 4, work)
        seg = lax.dynamic_index_in_dim(seg, lax.axis_index("h"), 0, False)
        seg = lax.dynamic_index_in_dim(seg, lax.axis_index(("x", "c")), 1, False)
        seg = seg.astype(F32)

        row_index = jnp.arange(work, dtype=jnp.int32)
        allowed = (seg[:, :, None] == seg[:, None, :]) & (
            row_index[None, None, :] <= row_index[None, :, None]
        )
        position = jnp.sum(allowed.astype(F32), axis=-1) - 1.0
        half = HEAD_DIM // 2
        freq = rope_base ** (-(jnp.arange(half, dtype=F32) * 2.0) / HEAD_DIM)
        phase = position.reshape(-1)[:, None] * freq[None, :]
        cosine = jnp.concatenate([jnp.cos(phase)] * 2, axis=1)[:, None, :]
        sine = jnp.concatenate([jnp.sin(phase)] * 2, axis=1)[:, None, :]

        rows = nt * work
        work_rows = rows_bf.astype(F32)
        scale_one = lax.rsqrt(jnp.mean(work_rows * work_rows, axis=-1, keepdims=True) + epsilon)
        n_one = gather_t((work_rows * scale_one * gain_one).astype(BF16))
        qkv = dot(n_one, w_qkv)
        qw = GROUP * HEAD_DIM
        q = qkv[:, :qw].reshape(rows, GROUP, HEAD_DIM)
        k = qkv[:, qw : qw + HEAD_DIM].reshape(rows, 1, HEAD_DIM)
        v = qkv[:, qw + HEAD_DIM :].astype(BF16).reshape(nt, work, HEAD_DIM)
        q = (q * cosine + turn(q) * sine).astype(BF16).reshape(nt, work, GROUP, HEAD_DIM)
        k = (k * cosine + turn(k) * sine).astype(BF16).reshape(nt, work, HEAD_DIM)
        scores = jnp.einsum("bqgd,bkd->bgqk", q, k, preferred_element_type=F32) * factor
        scores = jnp.where(allowed[:, None], scores, -1e30)
        top = jnp.max(scores, axis=-1, keepdims=True)
        exps = jnp.exp(scores - top)
        prob = exps / jnp.sum(exps, axis=-1, keepdims=True)
        prob_bf = prob.astype(BF16)
        head_out = jnp.einsum("bgqk,bkd->bqgd", prob_bf, v, preferred_element_type=F32)
        head_out = head_out.reshape(rows, qw).astype(BF16)
        attn = scatter_t(dot(head_out, w_out))

        hidden = work_rows + attn
        scale_two = lax.rsqrt(jnp.mean(hidden * hidden, axis=-1, keepdims=True) + epsilon)
        n_two = gather_t((hidden * scale_two * gain_two).astype(BF16))
        cots = gather_t(grad_bf)
        gu_pre = dot(n_two, w_gu)
        gate, up = gu_pre[:, :ff], gu_pre[:, ff:]
        sig = jax.nn.sigmoid(gate)
        act = (gate * sig * up).astype(BF16)
        ffn = scatter_t(dot(act, w_down))
        delta = (attn + ffn).astype(BF16)

        d_act = dot_nt(cots, w_down)
        d_gate = (d_act * up * (sig * (1.0 + gate * (1.0 - sig)))).astype(BF16)
        d_up = (d_act * gate * sig).astype(BF16)
        d_gu = jnp.concatenate([d_gate, d_up], axis=1)
        d_n_two = scatter_t(dot_nt(d_gu, w_gu))
        g_down = dot_tn(act, cots).astype(BF16)
        g_gu = dot_tn(n_two, d_gu).astype(BF16)
        d_hidden, d_gain_two = norm_back(d_n_two, hidden, scale_two, gain_two)
        g_down = scatter_d(g_down).astype(F32)
        g_gu = own_rows(g_gu, gw).astype(F32)
        g_gate = ff_join(g_gu[:, :, :ff], ffb)
        g_up = ff_join(g_gu[:, :, ff:], ffb)

        d_attn = gather_t((grad_bf.astype(F32) + d_hidden).astype(BF16))
        g_out = dot_tn(head_out, d_attn).astype(BF16)
        g_out = lax.ppermute(scatter_d(g_out), ALL, unperm).astype(F32)
        d_head = dot_nt(d_attn, w_out).astype(BF16).reshape(nt, work, GROUP, HEAD_DIM)
        d_prob = jnp.einsum("bqgd,bkd->bgqk", d_head, v, preferred_element_type=F32)
        d_v = jnp.einsum("bgqk,bqgd->bkd", prob_bf, d_head, preferred_element_type=F32)
        d_s = prob * (d_prob - jnp.sum(prob * d_prob, axis=-1, keepdims=True))
        d_s = d_s.astype(BF16)
        d_q = jnp.einsum("bgqk,bkd->bqgd", d_s, k, preferred_element_type=F32) * factor
        d_k = jnp.einsum("bgqk,bqgd->bkd", d_s, q, preferred_element_type=F32) * factor
        d_q = d_q.reshape(rows, GROUP, HEAD_DIM)
        d_k = d_k.reshape(rows, 1, HEAD_DIM)
        d_q = (d_q * cosine + turn_back(d_q * sine)).astype(BF16).reshape(rows, qw)
        d_k = (d_k * cosine + turn_back(d_k * sine)).astype(BF16).reshape(rows, HEAD_DIM)
        d_v = d_v.astype(BF16).reshape(rows, HEAD_DIM)
        d_qkv = jnp.concatenate([d_q, d_k, d_v], axis=1)
        d_n_one = scatter_t(dot_nt(d_qkv, w_qkv))
        g_qkv = own_rows(dot_tn(n_one, d_qkv).astype(BF16), gw).astype(F32)
        g_qkv = jnp.transpose(g_qkv, (1, 0, 2))
        g_query = g_qkv[:, :, :qw].reshape(gw, -1)
        g_key = g_qkv[:, :, qw : qw + HEAD_DIM].reshape(gw, -1)
        g_value = g_qkv[:, :, qw + HEAD_DIM :].reshape(gw, -1)
        d_norm, d_gain_one = norm_back(d_n_one, work_rows, scale_one, gain_one)
        back = (d_norm + d_hidden).astype(BF16)

        slot_delta = jnp.zeros((slots, width), BF16).at[recv_slot].set(delta)
        slot_back = jnp.zeros((slots, width), BF16).at[recv_slot].set(back)
        d_gains = jnp.concatenate([d_gain_one.reshape(n, gw), d_gain_two.reshape(n, gw)], axis=1)
        d_gains = lax.all_to_all(d_gains, ALL, split_axis=0, concat_axis=0, tiled=True)
        d_gains = jnp.sum(d_gains, axis=0)
        got_delta = lax.all_to_all(slot_delta, ALL, split_axis=0, concat_axis=0, tiled=True)
        got_back = lax.all_to_all(slot_back, ALL, split_axis=0, concat_axis=0, tiled=True)
        local_delta = jnp.zeros(tokens.shape, BF16).at[send_row].set(got_delta, mode="drop")
        local_back = jnp.zeros(tokens.shape, BF16).at[send_row].set(got_back, mode="drop")
        output = (tokens.astype(F32) + local_delta.astype(F32)).astype(BF16)
        input_grad = (cotangent.astype(F32) + local_back.astype(F32)).astype(BF16)
        return (
            output,
            input_grad,
            g_query,
            g_key,
            g_value,
            g_out,
            d_gains[:gw],
            g_gate,
            g_up,
            g_down,
            d_gains[gw:],
        )

    return shards


def solution(mesh):
    n = mesh.devices.size
    grid = Mesh(mesh.devices.reshape(n // 16, 2, 2, 2, 2), ALL)
    two, one = P(ALL, None), P(ALL)
    return jax.shard_map(
        make(n),
        mesh=grid,
        in_specs=(two, two, one, one, one, two, two, two, two, one, two, two, two, one),
        out_specs=(two, two, two, two, two, two, one, two, two, two, one),
        check_vma=False,
    )
```

```python
import jax
import jax.numpy as jnp
from jax import lax
from jax.experimental import pallas as pl
from jax.experimental.pallas import tpu as pltpu
from jax.sharding import Mesh, PartitionSpec as P

QUERY_HEADS = 16
KEY_VALUE_HEADS = 4
HEAD_DIM = 128
GROUP = QUERY_HEADS // KEY_VALUE_HEADS

epsilon = 1e-05
rope_base = 10000.0

ALL = ("h", "l", "y", "x", "c")
FOUR = ("l", "y")
LINE = ("h", "l")
GROUP_F = ("h", "l", "y")
F32 = jnp.float32
BF16 = jnp.bfloat16


def dot(left, right):
    return jnp.dot(left, right, preferred_element_type=F32)


def dot_tn(left, right):
    return lax.dot_general(left, right, (((0,), (0,)), ((), ())), preferred_element_type=F32)


def dot_nt(left, right):
    return lax.dot_general(left, right, (((1,), (1,)), ((), ())), preferred_element_type=F32)


def swap(block, axis):
    return lax.ppermute(block, axis, [(0, 1), (1, 0)])


def shift(block, size):
    return lax.ppermute(block, LINE, [(i, (i + 1) % size) for i in range(size)])


def pair(block, other, axis):
    first = lax.axis_index(axis) == 0
    return jnp.stack([jnp.where(first, block, other), jnp.where(first, other, block)])


def add(*parts):
    return sum(p.astype(F32) for p in parts).astype(BF16)


class Order:
    def __init__(self, token):
        self.token = token

    def step(self, *values):
        values = lax.optimization_barrier((*values, self.token))
        self.token = values[-1]
        return values[:-1] if len(values) > 2 else values[0]


def split_columns(gate, up, parts):
    rows, cols = gate.shape
    w = cols // parts

    def kernel(g_ref, u_ref, o_ref):
        for j in range(parts):
            o_ref[j, :, :w] = g_ref[:, j * w : (j + 1) * w]
            o_ref[j, :, w:] = u_ref[:, j * w : (j + 1) * w]

    return pl.pallas_call(
        kernel,
        out_shape=jax.ShapeDtypeStruct((parts, rows, 2 * w), BF16),
        name="split_columns",
    )(gate, up)


def join_columns(blocks):
    parts, rows, w = blocks.shape
    w = w // 2

    def kernel(b_ref, g_ref, u_ref):
        for j in range(parts):
            g_ref[:, j * w : (j + 1) * w] = b_ref[j, :, :w].astype(F32)
            u_ref[:, j * w : (j + 1) * w] = b_ref[j, :, w:].astype(F32)

    out = jax.ShapeDtypeStruct((rows, parts * w), F32)
    return pl.pallas_call(kernel, out_shape=(out, out), name="join_columns")(blocks)


QW = GROUP * HEAD_DIM
FACTOR = HEAD_DIM ** (-0.5)


def rotate(values, cosine, sine):
    return values * cosine + pltpu.roll(values, HEAD_DIM // 2, 1) * sine


def probabilities(q, k, seg_col, seg_row):
    work = k.shape[0]
    row = lax.broadcasted_iota(jnp.int32, (work, work), 0)
    col = lax.broadcasted_iota(jnp.int32, (work, work), 1)
    allowed = (seg_col == seg_row) & (col <= row)
    allowed = jnp.concatenate([allowed.astype(F32)] * GROUP, axis=0) > 0.5
    scores = jnp.where(allowed, dot_nt(q, k) * FACTOR, -1e30)
    exps = jnp.exp(scores - jnp.max(scores, axis=-1, keepdims=True))
    return exps / jnp.sum(exps, axis=-1, keepdims=True)


def stack_heads(values):
    return jnp.concatenate([values[:, i * HEAD_DIM : (i + 1) * HEAD_DIM] for i in range(GROUP)], axis=0)


def lay_heads(values):
    work = values.shape[0] // GROUP
    return jnp.concatenate([values[i * work : (i + 1) * work] for i in range(GROUP)], axis=1)


def attention_forward(qkv, cosine, sine, seg_col, seg_row, blocks):
    rows = qkv.shape[0]
    work = rows // blocks

    def kernel(x_ref, c_ref, s_ref, sc_ref, sr_ref, o_ref, r_ref):
        c, s = c_ref[...], s_ref[...]
        heads = [rotate(x_ref[:, i * HEAD_DIM : (i + 1) * HEAD_DIM], c, s) for i in range(GROUP + 1)]
        q = jnp.concatenate(heads[:GROUP], axis=0).astype(BF16)
        k = heads[GROUP].astype(BF16)
        v = x_ref[:, QW + HEAD_DIM :].astype(BF16)
        prob = probabilities(q, k, sc_ref[0], sr_ref[0])
        o_ref[...] = lay_heads(dot(prob.astype(BF16), v)).astype(BF16)
        for i in range(GROUP):
            r_ref[:, i * HEAD_DIM : (i + 1) * HEAD_DIM] = heads[i].astype(BF16)
        r_ref[:, QW : QW + HEAD_DIM] = k
        r_ref[:, QW + HEAD_DIM :] = v

    def block(cols):
        return pl.BlockSpec((work, cols), lambda i: (i, 0))

    return pl.pallas_call(
        kernel,
        grid=(blocks,),
        in_specs=[
            block(QW + 2 * HEAD_DIM),
            block(HEAD_DIM),
            block(HEAD_DIM),
            pl.BlockSpec((1, work, 1), lambda i: (i, 0, 0)),
            pl.BlockSpec((1, 1, work), lambda i: (i, 0, 0)),
        ],
        out_specs=[block(QW), block(QW + 2 * HEAD_DIM)],
        out_shape=[
            jax.ShapeDtypeStruct((rows, QW), BF16),
            jax.ShapeDtypeStruct((rows, QW + 2 * HEAD_DIM), BF16),
        ],
        name="attention_forward",
    )(qkv, cosine, sine, seg_col, seg_row)


def attention_backward(d_head, turned, cosine, sine, seg_col, seg_row, blocks):
    rows = d_head.shape[0]
    work = rows // blocks

    def kernel(d_ref, r_ref, c_ref, s_ref, sc_ref, sr_ref, o_ref):
        c, s = c_ref[...], -s_ref[...]
        q = stack_heads(r_ref[:, :QW])
        k = r_ref[:, QW : QW + HEAD_DIM]
        v = r_ref[:, QW + HEAD_DIM :]
        d = stack_heads(d_ref[...])
        prob = probabilities(q, k, sc_ref[0], sr_ref[0])
        d_prob = dot_nt(d, v)
        d_v = dot_tn(prob.astype(BF16), d)
        d_s = prob * (d_prob - jnp.sum(prob * d_prob, axis=-1, keepdims=True))
        d_s = d_s.astype(BF16)
        d_q = dot(d_s, k) * FACTOR
        d_k = dot_tn(d_s, q) * FACTOR
        for i in range(GROUP):
            part = rotate(d_q[i * work : (i + 1) * work], c, s)
            o_ref[:, i * HEAD_DIM : (i + 1) * HEAD_DIM] = part.astype(BF16)
        o_ref[:, QW : QW + HEAD_DIM] = rotate(d_k, c, s).astype(BF16)
        o_ref[:, QW + HEAD_DIM :] = d_v.astype(BF16)

    def block(cols):
        return pl.BlockSpec((work, cols), lambda i: (i, 0))

    return pl.pallas_call(
        kernel,
        grid=(blocks,),
        in_specs=[
            block(QW),
            block(QW + 2 * HEAD_DIM),
            block(HEAD_DIM),
            block(HEAD_DIM),
            pl.BlockSpec((1, work, 1), lambda i: (i, 0, 0)),
            pl.BlockSpec((1, 1, work), lambda i: (i, 0, 0)),
        ],
        out_specs=block(QW + 2 * HEAD_DIM),
        out_shape=jax.ShapeDtypeStruct((rows, QW + 2 * HEAD_DIM), BF16),
        name="attention_backward",
    )(d_head, turned, cosine, sine, seg_col, seg_row)


def norm_back(grad_out, values_in, scale_rows, gain_row):
    scaled_grad = grad_out * gain_row
    grad_in = scale_rows * scaled_grad - values_in * scale_rows**3 * jnp.mean(
        scaled_grad * values_in, axis=-1, keepdims=True
    )
    grad_gain = jnp.sum(grad_out * values_in * scale_rows, axis=0)
    return (grad_in, grad_gain)


def make(n):
    nh = n // 16
    nt = 4
    nz = 2 * nh
    nu = 2 * nz

    head_bits = n // KEY_VALUE_HEADS
    perm = []
    for src in range(n):
        a, rest = divmod(src, head_bits)
        h, xc = divmod(rest, 4)
        perm.append((src, h * 16 + a * 4 + xc))
    unperm = [(b, a) for a, b in perm]

    def shards(
        tokens,
        cotangent,
        send_row,
        recv_slot,
        segment,
        query_weight,
        key_weight,
        value_weight,
        out_weight,
        attn_gain,
        gate_weight,
        up_weight,
        down_weight,
        ffn_gain,
    ):
        width = tokens.shape[1]
        work = recv_slot.shape[0]
        slots = send_row.shape[0]
        cap = slots // n
        gw = attn_gain.shape[0]
        ffb = down_weight.shape[0]
        ff = 4 * ffb
        half = work // 2
        extra = -(-max(2 * gw, work) // 128) * 128

        slot = jnp.arange(slots, dtype=jnp.int32)
        row_of_slot = jnp.full((slots,), work, jnp.int32).at[recv_slot].set(slot[:work])
        slot_of_row = jnp.full((tokens.shape[0],), slots, jnp.int32)
        slot_of_row = slot_of_row.at[send_row].set(slot, mode="drop")
        o = Order(slot_of_row)
        sync = o.step

        def to_all(rows):
            return lax.all_to_all(rows, ALL, split_axis=0, concat_axis=0, tiled=True)

        gains = jnp.concatenate([attn_gain, ffn_gain])
        ext = jnp.zeros((cap, extra), BF16)
        ext = ext.at[0, : 2 * gw].set(gains).at[1, :work].set(segment.astype(BF16))
        ext = jnp.broadcast_to(ext[None], (n, cap, extra)).reshape(slots, extra)
        out_rows = jnp.take(tokens, send_row, axis=0, mode="fill", fill_value=0)
        out_rows = jnp.concatenate([out_rows, ext], axis=1)

        heads = jnp.concatenate(
            [
                query_weight.reshape(gw, nt, QW),
                key_weight.reshape(gw, nt, HEAD_DIM),
                value_weight.reshape(gw, nt, HEAD_DIM),
            ],
            axis=2,
        )
        heads = jnp.transpose(heads, (1, 0, 2))
        heads = lax.all_to_all(heads, FOUR, split_axis=0, concat_axis=0, tiled=True)
        perm_out = lax.ppermute(out_weight, ALL, perm)
        heads, perm_out, out_rows, cotangent, gate_weight, up_weight = sync(
            heads, perm_out, out_rows, cotangent, gate_weight, up_weight
        )
        come = to_all(out_rows)
        heads = heads.reshape(nt * gw, -1)
        out_cots = jnp.take(cotangent, send_row, axis=0, mode="fill", fill_value=0)
        gu = split_columns(gate_weight, up_weight, nu)
        if nh == 2:
            qkv_h, out_h = swap(heads, "h"), swap(perm_out, "h")
            qkv_h, out_h, out_cots, gu = sync(qkv_h, out_h, out_cots, gu)
            qkv_h, out_h = pair(heads, qkv_h, "h"), pair(perm_out, out_h, "h")
        else:
            qkv_h = lax.all_gather(heads, "h", axis=0, tiled=False)
            out_h = lax.all_gather(perm_out, "h", axis=0, tiled=False)
        qkv_h, out_h = sync(qkv_h, out_h)
        w_qkv = lax.all_gather(qkv_h.reshape(nh * nt * gw, -1), ("x", "c"), axis=0, tiled=True)
        w_out = lax.all_gather(out_h.reshape(nh * gw, -1), ("x", "c"), axis=0, tiled=True)
        come = sync(come)

        rows_bf = jnp.take(come[:, :width], recv_slot, axis=0)
        ext = come[:, width:].reshape(n, cap, extra)
        gain_one = ext[:, 0, :gw].reshape(n * gw).astype(F32)
        gain_two = ext[:, 0, gw : 2 * gw].reshape(n * gw).astype(F32)
        work_rows = rows_bf.astype(F32)
        scale_one = lax.rsqrt(jnp.mean(work_rows * work_rows, axis=-1, keepdims=True) + epsilon)
        n_own = sync((work_rows * scale_one * gain_one).astype(BF16))

        row_l, row_y = swap(n_own, "l"), swap(n_own, "y")
        ext = sync(ext)
        me = lax.axis_index(ALL)
        seg = jnp.take(ext[:, 1, :work], jnp.stack([me, me ^ 8, me ^ 4, me ^ 12]), axis=0)
        seg = seg.astype(F32)
        row_index = jnp.arange(work, dtype=jnp.int32)
        allowed = (seg[:, :, None] == seg[:, None, :]) & (
            row_index[None, None, :] <= row_index[None, :, None]
        )
        position = jnp.sum(allowed.astype(F32), axis=-1) - 1.0
        freq = rope_base ** (-(jnp.arange(HEAD_DIM // 2, dtype=F32) * 2.0) / HEAD_DIM)
        phase = position.reshape(-1)[:, None] * freq[None, :]
        cosine = jnp.concatenate([jnp.cos(phase)] * 2, axis=1)
        sine = jnp.concatenate([-jnp.sin(phase), jnp.sin(phase)], axis=1)
        seg_col, seg_row = seg[:, :, None], seg[:, None, :]
        row_l, row_y, sine, cosine, seg_col, seg_row = sync(
            row_l, row_y, sine, cosine, seg_col, seg_row
        )
        row_ly = swap(row_y[:half], "l"), swap(row_l[half:], "y")
        w_qkv = w_qkv.reshape(4, nh * nt, gw, -1)
        w_qkv = jnp.transpose(w_qkv, (1, 0, 2, 3)).reshape(width, -1)
        row_ly, w_qkv, out_cots = sync(row_ly, w_qkv, out_cots)
        come_cots = to_all(out_cots)
        w_out = w_out.reshape(4, nh, gw, -1)
        w_out = jnp.transpose(w_out, (1, 0, 2, 3)).reshape(QW, width)
        n_one = jnp.concatenate([n_own, row_l, row_y, row_ly[0], row_ly[1]], axis=0)

        qkv = sync(dot(n_one, w_qkv))
        head_out, turned = attention_forward(qkv, cosine, sine, seg_col, seg_row, nt)
        head_out, turned = sync(head_out, turned)

        def sum_four(part, first, second):
            p = [part[i * work : (i + 1) * work] for i in range(4)]
            low, high = swap(p[3][:half], "l"), swap(p[3][half:], "y")
            (low, high), beside = sync((low, high), first())
            by = jnp.concatenate([add(p[2][:half], low), p[2][half:]], axis=0)
            bl = jnp.concatenate([p[1][:half], add(p[1][half:], high)], axis=0)
            by, bl = sync(by, bl)
            by, bl = swap(by, "y"), swap(bl, "l")
            (by, bl), beside = sync((by, bl), second(beside))
            return p[0].astype(F32) + bl.astype(F32) + by.astype(F32), beside

        part, come_cots, gu = sync(dot(head_out, w_out).astype(BF16), come_cots, gu)
        gu = lax.all_to_all(gu, GROUP_F, split_axis=0, concat_axis=0, tiled=True)
        grad_bf = jnp.take(come_cots, recv_slot, axis=0)
        w_down = lax.all_gather(down_weight, ("x", "c"), axis=0, tiled=True)
        attn, (gu, w_down) = sum_four(part, lambda: work_rows, lambda e: (gu, w_down))
        w_gu = lax.all_gather(gu.reshape(nu * gw, -1), ("x", "c"), axis=0, tiled=True)
        w_gu = jnp.transpose(w_gu.reshape(4, nu, gw, -1), (1, 0, 2, 3)).reshape(width, -1)

        hidden = work_rows + attn
        scale_two = lax.rsqrt(jnp.mean(hidden * hidden, axis=-1, keepdims=True) + epsilon)
        n_own = (hidden * scale_two * gain_two).astype(BF16)
        both_z, both_y = [sync(jnp.concatenate([n_own, grad_bf], axis=0))], []

        def feed_forward(i):
            rows = jnp.concatenate([both_z[i][:work], both_y[i][:work]], axis=0)
            cots = jnp.concatenate([both_z[i][work:], both_y[i][work:]], axis=0)
            gu_pre = dot(rows, w_gu)
            pre, up = gu_pre[:, :ff], gu_pre[:, ff:]
            sig = jax.nn.sigmoid(pre)
            act = (pre * sig * up).astype(BF16)
            d_act = dot_nt(cots, w_down)
            d_gate = (d_act * up * (sig * (1.0 + pre * (1.0 - sig)))).astype(BF16)
            d_up = (d_act * pre * sig).astype(BF16)
            d_gu = jnp.concatenate([d_gate, d_up], axis=1)
            d_part, f_part = dot_nt(d_gu, w_gu).astype(BF16), dot(act, w_down).astype(BF16)
            own = jnp.concatenate([d_part[:work], f_part[:work]], axis=0)
            other = jnp.concatenate([d_part[work:], f_part[work:]], axis=0)
            return rows, cots, act, d_gu, own, other

        done = []
        for i in range(1, nz):
            nxt, oth = shift(both_z[-1], nz), swap(both_z[-1], "y")
            if i == 2:
                nxt, oth, w_gu = sync(nxt, oth, w_gu)
            elif i > 2:
                more = [feed_forward(j) for j in range(len(done), i - 1)]
                nxt, oth, more = sync(nxt, oth, more)
                done += more
            else:
                nxt, oth = sync(nxt, oth)
            both_z.append(nxt)
            both_y.append(oth)
        last = swap(both_z[-1], "y")
        last, more = sync(last, [feed_forward(j) for j in range(len(done), nz - 1)])
        both_y.append(last)
        done += more

        sent = swap(done[1][5], "y")
        done.append(sync(feed_forward(nz - 1)))
        own, other = [d[4] for d in done], [d[5] for d in done]
        n_two, cots, act, d_gu = (jnp.concatenate([d[k] for d in done], axis=0) for k in range(4))
        g_gu = dot_tn(n_two, d_gu).astype(BF16)
        g_gu = jnp.transpose(g_gu.reshape(nu, 4, gw, 2 * ff), (1, 0, 2, 3)).reshape(width, 2 * ff)
        g_gu, sent = sync(g_gu, sent)
        g_gu = lax.psum_scatter(g_gu, ("x", "c"), scatter_dimension=0, tiled=True)
        acc = sync(add(own[1], sent))
        for i in range(2, nz):
            acc, sent = shift(acc, nz), swap(other[i], "y")
            if i == 2:
                g_down = dot_tn(act, cots).astype(BF16)
                acc, sent, g_down = sync(acc, sent, g_down)
                g_down = lax.psum_scatter(g_down, ("x", "c"), scatter_dimension=0, tiled=True)
            else:
                acc, sent = sync(acc, sent)
            acc = sync(add(own[i], sent, acc))
        acc, sent, g_gu = sync(shift(acc, nz), swap(other[0], "y"), g_gu)
        total = own[0].astype(F32) + sent.astype(F32) + acc.astype(F32)
        d_hidden, d_gain_two = norm_back(total[:work], hidden, scale_two, gain_two)
        d_own = (grad_bf.astype(F32) + d_hidden).astype(BF16)
        delta = (attn + total[work:]).astype(BF16)
        d_hidden, d_own, delta = sync(d_hidden, d_own, delta)

        row_l, row_y = swap(d_own, "l"), swap(d_own, "y")
        slot_delta = jnp.take(delta, row_of_slot, axis=0, mode="fill", fill_value=0)
        row_l, row_y, slot_delta = sync(row_l, row_y, slot_delta)
        row_ly = swap(row_y[:half], "l"), swap(row_l[half:], "y")
        row_ly, g_down = sync(row_ly, g_down)
        got_delta = to_all(slot_delta)
        d_attn = sync(jnp.concatenate([d_own, row_l, row_y, row_ly[0], row_ly[1]], axis=0))
        g_out = dot_tn(head_out, d_attn).astype(BF16)
        g_out = jnp.transpose(g_out.reshape(nh, 4, -1, width), (1, 0, 2, 3)).reshape(QW, width)
        g_out = sync(g_out)
        g_out = lax.psum_scatter(g_out, ("x", "c"), scatter_dimension=0, tiled=True)
        d_head = dot_nt(d_attn, w_out).astype(BF16)
        d_qkv = attention_backward(d_head, turned, cosine, sine, seg_col, seg_row, nt)
        d_qkv = sync(d_qkv)
        part, got_delta, g_gu = sync(dot_nt(d_qkv, w_qkv).astype(BF16), got_delta, g_gu)
        g_gu = lax.all_to_all(
            g_gu.reshape(nu, gw, -1), GROUP_F, split_axis=0, concat_axis=0, tiled=True
        )

        def first():
            g = dot_tn(n_one, d_qkv).astype(BF16)
            g = jnp.transpose(g.reshape(nu, 4, gw, -1), (1, 0, 2, 3))
            return g.reshape(width, -1)

        def add_h(summed):
            if nh != 2:
                return lax.psum_scatter(summed, "h", scatter_dimension=0, tiled=True)
            i = lax.axis_index("h")
            both = summed.reshape(2, -1, summed.shape[1])
            mine = lax.dynamic_index_in_dim(both, i, 0, False)
            other = lax.dynamic_index_in_dim(both, 1 - i, 0, False)
            return add(mine, swap(other, "h"))

        held = {}

        def second(g):
            held["qkv"] = lax.psum_scatter(g, ("x", "c"), scatter_dimension=0, tiled=True)
            local = jnp.take(got_delta, o.token, axis=0, mode="fill", fill_value=0)
            output = (tokens.astype(F32) + local.astype(F32)).astype(BF16)
            return add_h(g_out), join_columns(g_gu), output

        d_n_one, (g_out, (g_gate, g_up), output) = sum_four(part, first, second)
        g_qkv = held["qkv"]
        d_norm, d_gain_one = norm_back(d_n_one, work_rows, scale_one, gain_one)
        back = (d_norm + d_hidden).astype(BF16)

        d_gains = jnp.concatenate([d_gain_one.reshape(n, gw), d_gain_two.reshape(n, gw)], axis=1)
        high = d_gains.astype(BF16)
        low = (d_gains - high.astype(F32)).astype(BF16)
        pad = jnp.zeros((n, cap - 2, 2 * gw), BF16)
        d_gains = jnp.concatenate([high[:, None], low[:, None], pad], axis=1)
        d_gains = jnp.pad(d_gains, ((0, 0), (0, 0), (0, extra - 2 * gw))).reshape(slots, extra)
        slot_back = jnp.take(back, row_of_slot, axis=0, mode="fill", fill_value=0)
        slot_back = sync(jnp.concatenate([slot_back, d_gains], axis=1))
        got_back = to_all(slot_back)
        g_out = lax.ppermute(g_out, ALL, unperm)
        got_back, g_qkv = sync(got_back, add_h(sync(g_qkv)))
        g_qkv = g_qkv.reshape(nt, gw, -1)
        t_me = lax.axis_index(FOUR)
        own, to_l, to_y, to_ly = sync(
            *(lax.dynamic_index_in_dim(g_qkv, t_me ^ r, 0, False) for r in (0, 2, 1, 3))
        )
        to_l, to_y = swap(to_l, "l"), swap(to_y, "y")
        to_ly = lax.ppermute(to_ly, FOUR, [(i, 3 - i) for i in range(4)])
        d_gains = got_back[:, width:].reshape(n, cap, extra)[:, :2, : 2 * gw]
        d_gains = jnp.sum(d_gains.astype(F32), axis=(0, 1))
        local_back = jnp.take(got_back[:, :width], o.token, axis=0, mode="fill", fill_value=0)
        input_grad = (cotangent.astype(F32) + local_back.astype(F32)).astype(BF16)
        g_down = g_down.astype(F32)
        g_out = g_out.astype(F32)
        own, to_l, to_y, to_ly, g_out, g_down, input_grad = sync(
            own, to_l, to_y, to_ly, g_out, g_down, input_grad
        )
        g_qkv = pair(pair(own, to_y, "y"), pair(to_l, to_ly, "y"), "l").reshape(nt, gw, -1)
        g_qkv = jnp.transpose(g_qkv.astype(F32), (1, 0, 2))
        g_query = g_qkv[:, :, :QW].reshape(gw, -1)
        g_key = g_qkv[:, :, QW : QW + HEAD_DIM].reshape(gw, -1)
        g_value = g_qkv[:, :, QW + HEAD_DIM :].reshape(gw, -1)
        return (
            output,
            input_grad,
            g_query,
            g_key,
            g_value,
            g_out,
            d_gains[:gw],
            g_gate,
            g_up,
            g_down,
            d_gains[gw:],
        )

    return shards


def solution(mesh):
    n = mesh.devices.size
    grid = Mesh(mesh.devices.reshape(n // 16, 2, 2, 2, 2), ALL)
    two, one = P(ALL, None), P(ALL)
    return jax.shard_map(
        make(n),
        mesh=grid,
        in_specs=(two, two, one, one, one, two, two, two, two, one, two, two, two, one),
        out_specs=(two, two, two, two, two, two, one, two, two, two, one),
        check_vma=False,
    )
```

```python
import jax
import jax.numpy as jnp
from jax import lax
from jax.experimental import pallas as pl
from jax.experimental.pallas import tpu as pltpu
from jax.sharding import Mesh, PartitionSpec as P

QUERY_HEADS = 16
KEY_VALUE_HEADS = 4
HEAD_DIM = 128
GROUP = QUERY_HEADS // KEY_VALUE_HEADS

epsilon = 1e-05
rope_base = 10000.0

ALL = ("h", "l", "y", "x", "c")
FOUR = ("l", "y")
LINE = ("h", "l")
GROUP_F = ("h", "l", "y")
F32 = jnp.float32
BF16 = jnp.bfloat16


def dot(left, right):
    return jnp.dot(left, right, preferred_element_type=F32)


def dot_tn(left, right):
    return lax.dot_general(left, right, (((0,), (0,)), ((), ())), preferred_element_type=F32)


def dot_nt(left, right):
    return lax.dot_general(left, right, (((1,), (1,)), ((), ())), preferred_element_type=F32)


def swap(block, axis):
    return lax.ppermute(block, axis, [(0, 1), (1, 0)])


def shift(block, size):
    return lax.ppermute(block, LINE, [(i, (i + 1) % size) for i in range(size)])


def pair(block, other, axis):
    first = lax.axis_index(axis) == 0
    return jnp.stack([jnp.where(first, block, other), jnp.where(first, other, block)])


def pick(blocks, axis):
    i = lax.axis_index(axis)
    mine = lax.dynamic_index_in_dim(blocks, i, 0, False)
    return mine, lax.dynamic_index_in_dim(blocks, 1 - i, 0, False)


def add(*parts):
    return sum(p.astype(F32) for p in parts).astype(BF16)


class Order:
    def __init__(self, token):
        self.token = token

    def step(self, *values):
        values = lax.optimization_barrier((*values, self.token))
        self.token = values[-1]
        return values[:-1] if len(values) > 2 else values[0]


def lanes(w):
    main = w // 128 * 128
    gate = ((slice(0, main), slice(0, main)), (slice(main, w), slice(2 * main, main + w)))
    up = ((slice(0, main), slice(main, 2 * main)), (slice(main, w), slice(main + w, 2 * w)))
    return gate, up


def split_columns(gate, up, parts):
    rows, cols = gate.shape
    w = cols // parts

    def kernel(g_ref, u_ref, o_ref):
        for j in range(parts):
            for ref, places in zip((g_ref, u_ref), lanes(w)):
                for at, to in places:
                    o_ref[j, :, to] = ref[:, j * w + at.start : j * w + at.stop]

    return pl.pallas_call(
        kernel,
        out_shape=jax.ShapeDtypeStruct((parts, rows, 2 * w), BF16),
        name="split_columns",
    )(gate, up)


def join_columns(blocks):
    parts, rows, w = blocks.shape
    w = w // 2

    def kernel(b_ref, g_ref, u_ref):
        for j in range(parts):
            for ref, places in zip((g_ref, u_ref), lanes(w)):
                for at, to in places:
                    ref[:, j * w + at.start : j * w + at.stop] = b_ref[j, :, to].astype(F32)

    out = jax.ShapeDtypeStruct((rows, parts * w), F32)
    return pl.pallas_call(kernel, out_shape=(out, out), name="join_columns")(blocks)


BESIDE = pl.CostEstimate(flops=1, bytes_accessed=1, transcendentals=0)


def feed_forward(first, second, w_gu, w_down):
    work, width = first.shape[0] // 2, first.shape[1]
    w = w_down.shape[0]

    def kernel(a_ref, b_ref, r_ref, d_ref, act_ref, dgu_ref, own_ref, other_ref, g_ref):
        in_order(r_ref, g_ref)
        rows = jnp.concatenate([a_ref[:work], b_ref[:work]], axis=0)
        cots = jnp.concatenate([a_ref[work:], b_ref[work:]], axis=0)
        pre = dot(rows, g_ref[...])
        d_act = dot_nt(cots, d_ref[...])
        for (at, g), (_, u) in zip(*lanes(w)):
            if at.start == at.stop:
                continue
            gate, up, d = pre[:, g], pre[:, u], d_act[:, at]
            sig = 1.0 / (1.0 + jnp.exp(-gate))
            silu = gate * sig
            act_ref[:, at] = (silu * up).astype(BF16)
            dgu_ref[:, g] = (d * up * (sig * (1.0 + gate * (1.0 - sig)))).astype(BF16)
            dgu_ref[:, u] = (d * silu).astype(BF16)
        back = dot_nt(dgu_ref[...], g_ref[...]).astype(BF16)
        own_ref[:work], other_ref[:work] = back[:work], back[work:]
        out = dot(act_ref[...], d_ref[...]).astype(BF16)
        own_ref[work:], other_ref[work:] = out[:work], out[work:]

    def shape(cols):
        return jax.ShapeDtypeStruct((2 * work, cols), BF16)

    return pl.pallas_call(
        kernel,
        out_shape=(shape(w), shape(2 * w), shape(width), shape(width)),
        scratch_shapes=[pltpu.VMEM((width, 2 * w), BF16)],
        cost_estimate=BESIDE,
        name="feed_forward",
    )(first, second, w_gu, w_down)


def shared_gradient(lefts, rights, share, rows):
    count, each = len(rights), len(lefts) // len(rights)
    height, width = rights[0].shape[0], lefts[0].shape[1]
    cols = rights[0].shape[1]
    each_step = max(1, 256 // (share * rows))
    step = share * rows * each_step

    def kernel(*refs):
        ins, o_ref = refs[:-1], refs[-1]
        total = None
        for i in range(count):
            left = [ins[i * each + j][...] for j in range(each)]
            left = left[0] if each == 1 else jnp.concatenate(left, axis=0)
            part = dot_tn(left, ins[count * each + i][...])
            total = part if total is None else total + part
        for m in range(each_step):
            for i in range(share):
                at = (m * share + i) * rows
                o_ref[i, m] = total[at : at + rows].astype(BF16)

    left = pl.BlockSpec((height // each, step), lambda i: (0, i))
    right = pl.BlockSpec((height, cols), lambda i: (0, 0))
    return pl.pallas_call(
        kernel,
        grid=(width // step,),
        in_specs=[left] * (count * each) + [right] * count,
        out_specs=pl.BlockSpec((share, each_step, rows, cols), lambda i: (0, i, 0, 0)),
        out_shape=jax.ShapeDtypeStruct((share, width // step * each_step, rows, cols), BF16),
        cost_estimate=BESIDE,
        name="shared_gradient",
    )(*lefts, *rights).reshape(width, cols)


def down_gradient(acts, firsts, seconds):
    count = len(acts)
    work, width = firsts[0].shape[0] // 2, firsts[0].shape[1]
    w = acts[0].shape[1]
    step = 256

    def kernel(*refs):
        ins, o_ref = refs[:-1], refs[-1]
        total = None
        for i in range(count):
            right = jnp.concatenate([ins[count + i][...], ins[2 * count + i][...]], axis=0)
            part = dot_tn(ins[i][...], right)
            total = part if total is None else total + part
        o_ref[...] = total.astype(BF16)

    left = pl.BlockSpec((2 * work, w), lambda i: (0, 0))
    right = pl.BlockSpec((work, step), lambda i: (1, i))
    return pl.pallas_call(
        kernel,
        grid=(width // step,),
        in_specs=[left] * count + [right] * (2 * count),
        out_specs=pl.BlockSpec((w, step), lambda i: (0, i)),
        out_shape=jax.ShapeDtypeStruct((w, width), BF16),
        cost_estimate=BESIDE,
        name="down_gradient",
    )(*acts, *firsts, *seconds)


QW = GROUP * HEAD_DIM
FACTOR = HEAD_DIM ** (-0.5)


def rotate(values, cosine, sine):
    return values * cosine + pltpu.roll(values, HEAD_DIM // 2, 1) * sine


def probabilities(q, k, seg_col, seg_row):
    work = k.shape[0]
    row = lax.broadcasted_iota(jnp.int32, (work, work), 0)
    col = lax.broadcasted_iota(jnp.int32, (work, work), 1)
    allowed = (seg_col == seg_row) & (col <= row)
    allowed = jnp.concatenate([allowed.astype(F32)] * GROUP, axis=0) > 0.5
    scores = jnp.where(allowed, dot_nt(q, k) * FACTOR, -1e30)
    exps = jnp.exp(scores - jnp.max(scores, axis=-1, keepdims=True))
    return exps / jnp.sum(exps, axis=-1, keepdims=True)


def stack_heads(values):
    return jnp.concatenate([values[:, i * HEAD_DIM : (i + 1) * HEAD_DIM] for i in range(GROUP)], axis=0)


def lay_heads(values):
    work = values.shape[0] // GROUP
    return jnp.concatenate([values[i * work : (i + 1) * work] for i in range(GROUP)], axis=1)


def in_order(from_ref, to_ref):
    share, members, rows = from_ref.shape[:3]
    for i in range(share):
        for m in range(members):
            at = (m * share + i) * rows
            to_ref[at : at + rows, :] = from_ref[i, m]


def four_shapes(work, width):
    full, half = (jax.ShapeDtypeStruct((r, width), BF16) for r in (work, work // 2))
    return (full, full, full, half, half)


def four_store(refs, values):
    at = 0
    for ref in refs:
        ref[...] = values[at : at + ref.shape[0]]
        at += ref.shape[0]


def four_load(refs, to_ref):
    at = 0
    for ref in refs:
        to_ref[at : at + ref.shape[0], :] = ref[...]
        at += ref.shape[0]


def attention_forward(pieces, w_qkv, w_out, cosine, sine, seg_col, seg_row, blocks):
    work, width = pieces[0].shape
    rows = work * blocks
    cols = QW + 2 * HEAD_DIM

    def kernel(*refs):
        gq_ref, go_ref, c_ref, s_ref, sc_ref, sr_ref, n_ref, o_ref, r_ref = refs[5:14]
        wq, wo, x_ref = refs[19:]
        four_load(refs[:5], n_ref)
        in_order(gq_ref, wq)
        x_ref[...] = dot(n_ref[...], wq[...])
        in_order(go_ref, wo)
        for b in range(blocks):
            at = slice(b * work, (b + 1) * work)
            c, s = c_ref[at], s_ref[at]
            heads = [rotate(x_ref[at, i * HEAD_DIM : (i + 1) * HEAD_DIM], c, s) for i in range(GROUP + 1)]
            q = jnp.concatenate(heads[:GROUP], axis=0).astype(BF16)
            k = heads[GROUP].astype(BF16)
            v = x_ref[at, QW + HEAD_DIM :].astype(BF16)
            prob = probabilities(q, k, sc_ref[b], sr_ref[b])
            o_ref[at] = lay_heads(dot(prob.astype(BF16), v)).astype(BF16)
            for i in range(GROUP):
                r_ref[at, i * HEAD_DIM : (i + 1) * HEAD_DIM] = heads[i].astype(BF16)
            r_ref[at, QW : QW + HEAD_DIM] = k
            r_ref[at, QW + HEAD_DIM :] = v
        four_store(refs[14:19], dot(o_ref[...], wo[...]).astype(BF16))

    return pl.pallas_call(
        kernel,
        out_shape=(
            jax.ShapeDtypeStruct((rows, width), BF16),
            jax.ShapeDtypeStruct((rows, QW), BF16),
            jax.ShapeDtypeStruct((rows, cols), BF16),
            *four_shapes(work, width),
        ),
        scratch_shapes=[
            pltpu.VMEM((width, cols), BF16),
            pltpu.VMEM((QW, width), BF16),
            pltpu.VMEM((rows, cols), F32),
        ],
        cost_estimate=BESIDE,
        name="attention_forward",
    )(*pieces, w_qkv, w_out, cosine, sine, seg_col, seg_row)


def attention_backward(
    pieces, w_out, w_qkv, n_one, head_out, turned, cosine, sine, seg_col, seg_row, blocks
):
    work, width = pieces[0].shape
    rows = work * blocks
    cols = QW + 2 * HEAD_DIM
    share, members, each = w_qkv.shape[:3]
    heads = w_out.shape[1]

    def kernel(*refs):
        go_ref, gq_ref, n_ref, a_ref, r_ref, c_ref, s_ref, sc_ref, sr_ref, k_ref, l_ref = refs[5:16]
        d_ref, o_ref, h_ref, wq, wo = refs[21:]
        four_load(refs[:5], d_ref)
        in_order(go_ref, wo)
        h_ref[...] = dot_nt(d_ref[...], wo[...]).astype(BF16)
        in_order(gq_ref, wq)
        for b in range(blocks):
            at = slice(b * work, (b + 1) * work)
            c, s = c_ref[at], -s_ref[at]
            q = stack_heads(r_ref[at, :QW])
            k = r_ref[at, QW : QW + HEAD_DIM]
            v = r_ref[at, QW + HEAD_DIM :]
            d = stack_heads(h_ref[at])
            prob = probabilities(q, k, sc_ref[b], sr_ref[b])
            d_prob = dot_nt(d, v)
            d_v = dot_tn(prob.astype(BF16), d)
            d_s = prob * (d_prob - jnp.sum(prob * d_prob, axis=-1, keepdims=True))
            d_s = d_s.astype(BF16)
            d_q = dot(d_s, k) * FACTOR
            d_k = dot_tn(d_s, q) * FACTOR
            for i in range(GROUP):
                part = rotate(d_q[i * work : (i + 1) * work], c, s)
                o_ref[at, i * HEAD_DIM : (i + 1) * HEAD_DIM] = part.astype(BF16)
            o_ref[at, QW : QW + HEAD_DIM] = rotate(d_k, c, s).astype(BF16)
            o_ref[at, QW + HEAD_DIM :] = d_v.astype(BF16)
        four_store(refs[16:21], dot_nt(o_ref[...], wq[...]).astype(BF16))
        step = share * each
        for m in range(members):
            grad = dot_tn(n_ref[:, m * step : (m + 1) * step], o_ref[...]).astype(BF16)
            for i in range(share):
                k_ref[i, m] = grad[i * each : (i + 1) * each]
        for m in range(heads):
            grad = dot_tn(a_ref[:, m * step : (m + 1) * step], d_ref[...]).astype(BF16)
            for i in range(share):
                l_ref[i, m] = grad[i * each : (i + 1) * each]

    return pl.pallas_call(
        kernel,
        out_shape=(
            jax.ShapeDtypeStruct((share, members, each, cols), BF16),
            jax.ShapeDtypeStruct((share, heads, each, width), BF16),
            *four_shapes(work, width),
        ),
        scratch_shapes=[
            pltpu.VMEM((rows, width), BF16),
            pltpu.VMEM((rows, cols), BF16),
            pltpu.VMEM((rows, QW), BF16),
            pltpu.VMEM((width, cols), BF16),
            pltpu.VMEM((QW, width), BF16),
        ],
        cost_estimate=BESIDE,
        name="attention_backward",
    )(*pieces, w_out, w_qkv, n_one, head_out, turned, cosine, sine, seg_col, seg_row)


def norm_back(grad_out, values_in, scale_rows, gain_row):
    scaled_grad = grad_out * gain_row
    grad_in = scale_rows * scaled_grad - values_in * scale_rows**3 * jnp.mean(
        scaled_grad * values_in, axis=-1, keepdims=True
    )
    grad_gain = jnp.sum(grad_out * values_in * scale_rows, axis=0)
    return (grad_in, grad_gain)


def make(n):
    nh = n // 16
    nt = 4
    nz = 2 * nh
    nu = 2 * nz

    head_bits = n // KEY_VALUE_HEADS
    perm = []
    for src in range(n):
        a, rest = divmod(src, head_bits)
        h, xc = divmod(rest, 4)
        perm.append((src, h * 16 + a * 4 + xc))
    unperm = [(b, a) for a, b in perm]

    def shards(
        tokens,
        cotangent,
        send_row,
        recv_slot,
        segment,
        query_weight,
        key_weight,
        value_weight,
        out_weight,
        attn_gain,
        gate_weight,
        up_weight,
        down_weight,
        ffn_gain,
    ):
        width = tokens.shape[1]
        work = recv_slot.shape[0]
        slots = send_row.shape[0]
        cap = slots // n
        gw = attn_gain.shape[0]
        ffb = down_weight.shape[0]
        ff = 4 * ffb
        half = work // 2
        extra = -(-max(2 * gw, work) // 128) * 128

        slot = jnp.arange(slots, dtype=jnp.int32)
        row_of_slot = jnp.full((slots,), work, jnp.int32).at[recv_slot].set(slot[:work])
        slot_of_row = jnp.full((tokens.shape[0],), slots, jnp.int32)
        slot_of_row = slot_of_row.at[send_row].set(slot, mode="drop")
        o = Order(slot_of_row)
        sync = o.step

        def rows_at(rows, index):
            last = rows.shape[0] - 1
            found = rows.at[jnp.minimum(index, last)].get(mode="promise_in_bounds")
            return jnp.where((index <= last)[:, None], found, jnp.zeros((), BF16))

        def to_all(rows):
            return lax.all_to_all(rows, ALL, split_axis=0, concat_axis=0, tiled=True)

        gains = jnp.concatenate([attn_gain, ffn_gain])
        ext = jnp.zeros((cap, extra), BF16)
        ext = ext.at[0, : 2 * gw].set(gains).at[1, :work].set(segment.astype(BF16))
        ext = jnp.broadcast_to(ext[None], (n, cap, extra)).reshape(slots, extra)
        out_rows = rows_at(tokens, send_row)
        out_rows = jnp.concatenate([out_rows, ext], axis=1)

        heads = jnp.concatenate(
            [
                query_weight.reshape(gw, nt, QW),
                key_weight.reshape(gw, nt, HEAD_DIM),
                value_weight.reshape(gw, nt, HEAD_DIM),
            ],
            axis=2,
        )
        heads = jnp.transpose(heads, (1, 0, 2))
        heads = lax.all_to_all(heads, FOUR, split_axis=0, concat_axis=0, tiled=True)
        perm_out = lax.ppermute(out_weight, ALL, perm)
        heads, perm_out, out_rows, cotangent, gate_weight, up_weight = sync(
            heads, perm_out, out_rows, cotangent, gate_weight, up_weight
        )
        heads = heads.reshape(nt * gw, -1)
        out_cots = rows_at(cotangent, send_row)
        gu = split_columns(gate_weight, up_weight, nu)
        if nh == 2:
            qkv_h = swap(heads, "h")
            heads, qkv_h, out_cots, gu, out_rows = sync(heads, qkv_h, out_cots, gu, out_rows)
            qkv_h = pair(heads, qkv_h, "h")
        else:
            out_cots, gu, out_rows = sync(out_cots, gu, out_rows)
            qkv_h = lax.all_gather(heads, "h", axis=0, tiled=False)
        come = to_all(out_rows)
        qkv_h = sync(qkv_h)
        w_qkv = lax.all_gather(qkv_h.reshape(nh * nt * gw, -1), ("x", "c"), axis=0, tiled=True)
        out_h = swap(perm_out, "h") if nh == 2 else perm_out
        come = sync(come)
        t_me = lax.axis_index(FOUR)

        rows_bf = jnp.take(come[:, :width], recv_slot, axis=0)
        ext = come[:, width:].reshape(n, cap, extra)
        gain_one = ext[:, 0, :gw].reshape(n * gw).astype(F32)
        gain_two = ext[:, 0, gw : 2 * gw].reshape(n * gw).astype(F32)
        work_rows = rows_bf.astype(F32)
        scale_one = lax.rsqrt(jnp.mean(work_rows * work_rows, axis=-1, keepdims=True) + epsilon)
        n_own = sync((work_rows * scale_one * gain_one).astype(BF16))

        row_l, row_y = swap(n_own, "l"), swap(n_own, "y")
        if nh == 2:
            out_h = pair(*sync(perm_out, out_h), "h")
        else:
            out_h = lax.all_gather(perm_out, "h", axis=0, tiled=False)
        out_h = sync(out_h)
        w_out = lax.all_gather(out_h.reshape(nh * gw, -1), ("x", "c"), axis=0, tiled=True)
        w_out = w_out.reshape(4, nh, gw, -1)
        ext = sync(ext)
        me = lax.axis_index(ALL)
        seg = jnp.take(ext[:, 1, :work], jnp.stack([me, me ^ 8, me ^ 4, me ^ 12]), axis=0)
        seg = seg.astype(F32)
        row_index = jnp.arange(work, dtype=jnp.int32)
        allowed = (seg[:, :, None] == seg[:, None, :]) & (
            row_index[None, None, :] <= row_index[None, :, None]
        )
        position = jnp.sum(allowed.astype(F32), axis=-1) - 1.0
        freq = rope_base ** (-(jnp.arange(HEAD_DIM // 2, dtype=F32) * 2.0) / HEAD_DIM)
        phase = position.reshape(-1)[:, None] * freq[None, :]
        cosine = jnp.concatenate([jnp.cos(phase)] * 2, axis=1)
        sine = jnp.concatenate([-jnp.sin(phase), jnp.sin(phase)], axis=1)
        seg_col, seg_row = seg[:, :, None], seg[:, None, :]
        row_l, row_y, sine, cosine, seg_col, seg_row = sync(
            row_l, row_y, sine, cosine, seg_col, seg_row
        )
        row_ly = swap(row_y[:half], "l"), swap(row_l[half:], "y")
        w_qkv = w_qkv.reshape(4, nh * nt, gw, -1)
        row_ly, w_qkv, out_cots = sync(row_ly, w_qkv, out_cots)
        come_cots = to_all(out_cots)
        n_one, head_out, turned, *part = attention_forward(
            (n_own, row_l, row_y, *row_ly), w_qkv, w_out, cosine, sine, seg_col, seg_row, nt
        )
        n_one, head_out, turned, part, gu = sync(n_one, head_out, turned, part, gu)

        def sum_four(part, first, second):
            p, bl, by, low, high = part
            low, high = swap(low, "l"), swap(high, "y")
            (low, high), beside = sync((low, high), first())
            by = lax.dynamic_update_slice(by, add(by[:half], low), (0, 0))
            bl = lax.dynamic_update_slice(bl, add(bl[half:], high), (half, 0))
            by, bl = sync(by, bl)
            by, bl = swap(by, "y"), swap(bl, "l")
            (by, bl), beside = sync((by, bl), second(beside))
            return p.astype(F32) + bl.astype(F32) + by.astype(F32), beside

        w_down = lax.all_gather(down_weight, ("x", "c"), axis=0, tiled=True)

        def beside_sum(gu):
            gu = lax.all_to_all(gu, GROUP_F, split_axis=0, concat_axis=0, tiled=True)
            return gu, w_down

        attn, (gu, w_down) = sum_four(part, lambda: sync(gu, come_cots)[0], beside_sum)
        grad_bf = jnp.take(come_cots, recv_slot, axis=0)
        w_gu = lax.all_gather(gu.reshape(nu * gw, -1), ("x", "c"), axis=0, tiled=True)
        w_gu = w_gu.reshape(4, nu, gw, -1)

        hidden = work_rows + attn
        scale_two = lax.rsqrt(jnp.mean(hidden * hidden, axis=-1, keepdims=True) + epsilon)
        n_own = (hidden * scale_two * gain_two).astype(BF16)
        both_z, both_y = [sync(jnp.concatenate([n_own, grad_bf], axis=0))], []

        done = {}
        for i in range(1, nz):
            nxt, oth = shift(both_z[-1], nz), swap(both_z[-1], "y")
            if i == nz - 1:
                nxt, oth, w_gu = sync(nxt, oth, w_gu)
            else:
                nxt, oth = sync(nxt, oth)
            both_z.append(nxt)
            both_y.append(oth)
        last = swap(both_z[-1], "y")

        def step(i):
            return feed_forward(both_z[i], both_y[i], w_gu, w_down)

        last, done[1], done[0] = sync(last, step(1), step(0))
        both_y.append(last)

        sent = swap(done[1][3], "y")
        sent, done[2] = sync(sent, step(2))
        acc = sync(add(done[1][2], sent))
        acc, sent = shift(acc, nz), swap(done[2][3], "y")
        for i in range(3, nz):
            done[i] = sync(step(i))
        done = [done[i] for i in range(nz)]
        acts, d_gus, own, other = ([d[k] for d in done] for k in range(4))
        lefts = [r for i in range(nz) for r in (both_z[i], both_y[i])]
        g_gu = shared_gradient(lefts, d_gus, 4, gw)
        g_gu, acc, sent = sync(g_gu, acc, sent)
        g_gu = lax.psum_scatter(g_gu, ("x", "c"), scatter_dimension=0, tiled=True)
        for i in range(2, nz):
            acc = sync(add(own[i], sent, acc))
            if i == nz - 1:
                break
            acc, sent = shift(acc, nz), swap(other[i + 1], "y")
            if i == 2:
                acc, sent, g_down = sync(acc, sent, down_gradient(acts, both_z, both_y))
                g_down = lax.psum_scatter(g_down, ("x", "c"), scatter_dimension=0, tiled=True)
            else:
                acc, sent = sync(acc, sent)
        acc, sent = sync(shift(acc, nz), swap(other[0], "y"))
        total = own[0].astype(F32) + sent.astype(F32) + acc.astype(F32)
        d_hidden, d_gain_two = norm_back(total[:work], hidden, scale_two, gain_two)
        d_own = (grad_bf.astype(F32) + d_hidden).astype(BF16)
        delta = (attn + total[work:]).astype(BF16)
        d_hidden, d_own, delta, g_gu = sync(d_hidden, d_own, delta, g_gu)

        row_l, row_y = swap(d_own, "l"), swap(d_own, "y")
        slot_delta = rows_at(delta, row_of_slot)
        g_gu = lax.all_to_all(
            g_gu.reshape(nu, gw, -1), GROUP_F, split_axis=0, concat_axis=0, tiled=True
        )
        row_l, row_y, slot_delta = sync(row_l, row_y, slot_delta)
        row_ly = sync(swap(row_y[:half], "l"), swap(row_l[half:], "y"))
        g_qkv, g_out, *part = attention_backward(
            (d_own, row_l, row_y, *row_ly),
            w_out,
            w_qkv,
            n_one,
            head_out,
            turned,
            cosine,
            sine,
            seg_col,
            seg_row,
            nt,
        )
        g_qkv, g_out, part = sync(g_qkv, g_out, part)
        g_qkv = lax.psum_scatter(
            g_qkv.reshape(width, -1), ("x", "c"), scatter_dimension=0, tiled=True
        )
        g_out, g_gu = sync(g_out, g_gu)
        g_out = jnp.swapaxes(g_out.reshape(2, 2, nh, gw, width), 0, 1)
        mine, other = sync(*pick(g_out, "c"))
        g_out = swap(other, "c")
        g_down, mine, g_out = sync(g_down, mine, g_out)
        mine, other = sync(*pick(add(mine, g_out), "x"))
        g_out = swap(other, "x")

        def add_h(blocks):
            if nh != 2:
                return lax.psum_scatter(blocks, "h", scatter_dimension=0, tiled=False)
            mine, other = pick(blocks, "h")
            return add(mine, swap(other, "h"))

        def beside_last(pair_x):
            summed = g_qkv.reshape(nh, nt * gw, -1)
            return add_h(summed), join_columns(g_gu), add_h(add(*pair_x))

        d_n_one, (g_qkv, (g_gate, g_up), g_out) = sum_four(part, lambda: (mine, g_out), beside_last)
        g_qkv = g_qkv.reshape(nt, gw, -1)
        own, to_l, to_y, to_ly = sync(
            *(lax.dynamic_index_in_dim(g_qkv, t_me ^ r, 0, False) for r in (0, 2, 1, 3))
        )
        to_l, to_y = swap(to_l, "l"), swap(to_y, "y")
        to_ly = lax.ppermute(to_ly, FOUR, [(i, 3 - i) for i in range(4)])
        g_out = lax.ppermute(g_out, ALL, unperm)
        d_norm, d_gain_one = norm_back(d_n_one, work_rows, scale_one, gain_one)
        back = (d_norm + d_hidden).astype(BF16)

        d_gains = jnp.concatenate([d_gain_one.reshape(n, gw), d_gain_two.reshape(n, gw)], axis=1)
        high = d_gains.astype(BF16)
        low = (d_gains - high.astype(F32)).astype(BF16)
        pad = jnp.zeros((n, cap - 2, 2 * gw), BF16)
        d_gains = jnp.concatenate([high[:, None], low[:, None], pad], axis=1)
        d_gains = jnp.pad(d_gains, ((0, 0), (0, 0), (0, extra - 2 * gw))).reshape(slots, extra)
        slot_back = rows_at(back, row_of_slot)
        slot_back = jnp.concatenate([slot_back, slot_delta, d_gains], axis=1)
        slot_back, own, to_l, to_y, to_ly, g_out = sync(slot_back, own, to_l, to_y, to_ly, g_out)
        got = to_all(slot_back)
        g_qkv = pair(pair(own, to_y, "y"), pair(to_l, to_ly, "y"), "l").reshape(nt, gw, -1)
        g_qkv = jnp.transpose(g_qkv.astype(F32), (1, 0, 2))
        g_down = g_down.astype(F32)
        g_out = g_out.astype(F32)
        g_qkv, g_down, g_out = sync(g_qkv, g_down, g_out)
        got = sync(got)
        d_gains = got[:, 2 * width :].reshape(n, cap, extra)[:, :2, : 2 * gw]
        d_gains = jnp.sum(d_gains.astype(F32), axis=(0, 1))
        local = rows_at(got, o.token)
        input_grad = (cotangent.astype(F32) + local[:, :width].astype(F32)).astype(BF16)
        output = (tokens.astype(F32) + local[:, width : 2 * width].astype(F32)).astype(BF16)
        g_query = g_qkv[:, :, :QW].reshape(gw, -1)
        g_key = g_qkv[:, :, QW : QW + HEAD_DIM].reshape(gw, -1)
        g_value = g_qkv[:, :, QW + HEAD_DIM :].reshape(gw, -1)
        return (
            output,
            input_grad,
            g_query,
            g_key,
            g_value,
            g_out,
            d_gains[:gw],
            g_gate,
            g_up,
            g_down,
            d_gains[gw:],
        )

    return shards


def solution(mesh):
    n = mesh.devices.size
    grid = Mesh(mesh.devices.reshape(n // 16, 2, 2, 2, 2), ALL)
    two, one = P(ALL, None), P(ALL)
    return jax.shard_map(
        make(n),
        mesh=grid,
        in_specs=(two, two, one, one, one, two, two, two, two, one, two, two, two, one),
        out_specs=(two, two, two, two, two, two, one, two, two, two, one),
        check_vma=False,
    )
```

```python
import jax
import jax.numpy as jnp
from jax import lax
from jax.experimental import pallas as pl
from jax.experimental.pallas import tpu as pltpu
from jax.sharding import Mesh, PartitionSpec as P

QUERY_HEADS = 16
KEY_VALUE_HEADS = 4
HEAD_DIM = 128
GROUP = QUERY_HEADS // KEY_VALUE_HEADS

epsilon = 1e-05
rope_base = 10000.0

ALL = ("h", "l", "y", "x", "c")
FOUR = ("l", "y")
LINE = ("h", "l")
GROUP_F = ("h", "l", "y")
F32 = jnp.float32
BF16 = jnp.bfloat16


def dot(left, right):
    return jnp.dot(left, right, preferred_element_type=F32)


def dot_tn(left, right):
    return lax.dot_general(left, right, (((0,), (0,)), ((), ())), preferred_element_type=F32)


def dot_nt(left, right):
    return lax.dot_general(left, right, (((1,), (1,)), ((), ())), preferred_element_type=F32)


def swap(block, axis):
    return lax.ppermute(block, axis, [(0, 1), (1, 0)])


def shift(block, size):
    return lax.ppermute(block, LINE, [(i, (i + 1) % size) for i in range(size)])


def pair(block, other, axis):
    first = lax.axis_index(axis) == 0
    return jnp.stack([jnp.where(first, block, other), jnp.where(first, other, block)])


def pick(blocks, axis):
    i = lax.axis_index(axis)
    mine = lax.dynamic_index_in_dim(blocks, i, 0, False)
    return mine, lax.dynamic_index_in_dim(blocks, 1 - i, 0, False)


def add(*parts):
    return sum(p.astype(F32) for p in parts).astype(BF16)


class Order:
    def __init__(self, token):
        self.token = token

    def step(self, *values):
        values = lax.optimization_barrier((*values, self.token))
        self.token = values[-1]
        return values[:-1] if len(values) > 2 else values[0]


def lanes(w):
    main = w // 128 * 128
    gate = ((slice(0, main), slice(0, main)), (slice(main, w), slice(2 * main, main + w)))
    up = ((slice(0, main), slice(main, 2 * main)), (slice(main, w), slice(main + w, 2 * w)))
    return gate, up


def split_columns(gate, up, parts):
    rows, cols = gate.shape
    w = cols // parts

    def kernel(g_ref, u_ref, o_ref):
        for j in range(parts):
            for ref, places in zip((g_ref, u_ref), lanes(w)):
                for at, to in places:
                    o_ref[j, :, to] = ref[:, j * w + at.start : j * w + at.stop]

    return pl.pallas_call(
        kernel,
        out_shape=jax.ShapeDtypeStruct((parts, rows, 2 * w), BF16),
        name="split_columns",
    )(gate, up)


def join_columns(blocks):
    parts, rows, w = blocks.shape
    w = w // 2

    def kernel(b_ref, g_ref, u_ref):
        for j in range(parts):
            for ref, places in zip((g_ref, u_ref), lanes(w)):
                for at, to in places:
                    ref[:, j * w + at.start : j * w + at.stop] = b_ref[j, :, to].astype(F32)

    out = jax.ShapeDtypeStruct((rows, parts * w), F32)
    return pl.pallas_call(kernel, out_shape=(out, out), name="join_columns")(blocks)


BESIDE = pl.CostEstimate(flops=1, bytes_accessed=1, transcendentals=0)


def feed_forward(first, second, w_gu, w_down):
    work, width = first.shape[0] // 2, first.shape[1]
    w = w_down.shape[0]
    parts = second if isinstance(second, tuple) else (second,)

    def kernel(a_ref, *refs):
        b_refs = refs[: len(parts)]
        r_ref, d_ref, act_ref, dgu_ref, own_ref, other_ref, g_ref = refs[len(parts) :]
        in_order(r_ref, g_ref)
        rows = jnp.concatenate([a_ref[:work], b_refs[0][:work]], axis=0)
        cots = jnp.concatenate([a_ref[work:], b_refs[-1][-work:]], axis=0)
        pre = dot(rows, g_ref[...])
        d_act = dot_nt(cots, d_ref[...])
        for (at, g), (_, u) in zip(*lanes(w)):
            if at.start == at.stop:
                continue
            gate, up, d = pre[:, g], pre[:, u], d_act[:, at]
            sig = 1.0 / (1.0 + jnp.exp(-gate))
            silu = gate * sig
            act_ref[:, at] = (silu * up).astype(BF16)
            dgu_ref[:, g] = (d * up * (sig * (1.0 + gate * (1.0 - sig)))).astype(BF16)
            dgu_ref[:, u] = (d * silu).astype(BF16)
        back = dot_nt(dgu_ref[...], g_ref[...]).astype(BF16)
        own_ref[:work], other_ref[:work] = back[:work], back[work:]
        out = dot(act_ref[...], d_ref[...]).astype(BF16)
        own_ref[work:], other_ref[work:] = out[:work], out[work:]

    def shape(cols):
        return jax.ShapeDtypeStruct((2 * work, cols), BF16)

    return pl.pallas_call(
        kernel,
        out_shape=(shape(w), shape(2 * w), shape(width), shape(width)),
        scratch_shapes=[pltpu.VMEM((width, 2 * w), BF16)],
        cost_estimate=BESIDE,
        name="feed_forward",
    )(first, *parts, w_gu, w_down)


def shared_gradient(lefts, rights, share, rows):
    count, each = len(rights), len(lefts) // len(rights)
    height, width = rights[0].shape[0], lefts[0].shape[1]
    cols = rights[0].shape[1]
    each_step = max(1, 256 // (share * rows))
    step = share * rows * each_step

    def kernel(*refs):
        ins, o_ref = refs[:-1], refs[-1]
        total = None
        for i in range(count):
            left = [ins[i * each + j][...] for j in range(each)]
            left = left[0] if each == 1 else jnp.concatenate(left, axis=0)
            part = dot_tn(left, ins[count * each + i][...])
            total = part if total is None else total + part
        for m in range(each_step):
            for i in range(share):
                at = (m * share + i) * rows
                o_ref[i, m] = total[at : at + rows].astype(BF16)

    left = pl.BlockSpec((height // each, step), lambda i: (0, i))
    right = pl.BlockSpec((height, cols), lambda i: (0, 0))
    return pl.pallas_call(
        kernel,
        grid=(width // step,),
        in_specs=[left] * (count * each) + [right] * count,
        out_specs=pl.BlockSpec((share, each_step, rows, cols), lambda i: (0, i, 0, 0)),
        out_shape=jax.ShapeDtypeStruct((share, width // step * each_step, rows, cols), BF16),
        cost_estimate=BESIDE,
        name="shared_gradient",
    )(*lefts, *rights).reshape(width, cols)


def down_gradient(acts, firsts, seconds):
    count = len(acts)
    work, width = firsts[0].shape[0] // 2, firsts[0].shape[1]
    w = acts[0].shape[1]
    step = 256

    def kernel(*refs):
        ins, o_ref = refs[:-1], refs[-1]
        total = None
        for i in range(count):
            right = jnp.concatenate([ins[count + i][...], ins[2 * count + i][...]], axis=0)
            part = dot_tn(ins[i][...], right)
            total = part if total is None else total + part
        o_ref[...] = total.astype(BF16)

    left = pl.BlockSpec((2 * work, w), lambda i: (0, 0))
    rights = [
        pl.BlockSpec((work, step), lambda i, at=r.shape[0] // work - 1: (at, i))
        for r in (*firsts, *seconds)
    ]
    return pl.pallas_call(
        kernel,
        grid=(width // step,),
        in_specs=[left] * count + rights,
        out_specs=pl.BlockSpec((w, step), lambda i: (0, i)),
        out_shape=jax.ShapeDtypeStruct((w, width), BF16),
        cost_estimate=BESIDE,
        name="down_gradient",
    )(*acts, *firsts, *seconds)


QW = GROUP * HEAD_DIM
FACTOR = HEAD_DIM ** (-0.5)


def rotate(values, cosine, sine):
    return values * cosine + pltpu.roll(values, HEAD_DIM // 2, 1) * sine


def probabilities(q, k, seg_col, seg_row):
    work = k.shape[0]
    row = lax.broadcasted_iota(jnp.int32, (work, work), 0)
    col = lax.broadcasted_iota(jnp.int32, (work, work), 1)
    allowed = (seg_col == seg_row) & (col <= row)
    allowed = jnp.concatenate([allowed.astype(F32)] * GROUP, axis=0) > 0.5
    scores = jnp.where(allowed, dot_nt(q, k) * FACTOR, -1e30)
    exps = jnp.exp(scores - jnp.max(scores, axis=-1, keepdims=True))
    return exps / jnp.sum(exps, axis=-1, keepdims=True)


def stack_heads(values):
    return jnp.concatenate([values[:, i * HEAD_DIM : (i + 1) * HEAD_DIM] for i in range(GROUP)], axis=0)


def lay_heads(values):
    work = values.shape[0] // GROUP
    return jnp.concatenate([values[i * work : (i + 1) * work] for i in range(GROUP)], axis=1)


def in_order(from_ref, to_ref):
    share, members, rows = from_ref.shape[:3]
    for i in range(share):
        for m in range(members):
            at = (m * share + i) * rows
            to_ref[at : at + rows, :] = from_ref[i, m]


def four_shapes(work, width):
    full, half = (jax.ShapeDtypeStruct((r, width), BF16) for r in (work, work // 2))
    return (full, full, full, half, half)


def four_store(refs, values):
    at = 0
    for ref in refs:
        ref[...] = values[at : at + ref.shape[0]]
        at += ref.shape[0]


def four_load(refs, to_ref):
    at = 0
    for ref in refs:
        to_ref[at : at + ref.shape[0], :] = ref[...]
        at += ref.shape[0]


def attention_forward(pieces, w_qkv, w_out, cosine, sine, seg_col, seg_row, blocks):
    work, width = pieces[0].shape
    rows = work * blocks
    cols = QW + 2 * HEAD_DIM

    def kernel(*refs):
        gq_ref, go_ref, c_ref, s_ref, sc_ref, sr_ref, n_ref, o_ref, r_ref = refs[5:14]
        wq, wo, x_ref = refs[19:]
        four_load(refs[:5], n_ref)
        in_order(gq_ref, wq)
        x_ref[...] = dot(n_ref[...], wq[...])
        in_order(go_ref, wo)
        for b in range(blocks):
            at = slice(b * work, (b + 1) * work)
            c, s = c_ref[at], s_ref[at]
            heads = [rotate(x_ref[at, i * HEAD_DIM : (i + 1) * HEAD_DIM], c, s) for i in range(GROUP + 1)]
            q = jnp.concatenate(heads[:GROUP], axis=0).astype(BF16)
            k = heads[GROUP].astype(BF16)
            v = x_ref[at, QW + HEAD_DIM :].astype(BF16)
            prob = probabilities(q, k, sc_ref[b], sr_ref[b])
            o_ref[at] = lay_heads(dot(prob.astype(BF16), v)).astype(BF16)
            for i in range(GROUP):
                r_ref[at, i * HEAD_DIM : (i + 1) * HEAD_DIM] = heads[i].astype(BF16)
            r_ref[at, QW : QW + HEAD_DIM] = k
            r_ref[at, QW + HEAD_DIM :] = v
        four_store(refs[14:19], dot(o_ref[...], wo[...]).astype(BF16))

    return pl.pallas_call(
        kernel,
        out_shape=(
            jax.ShapeDtypeStruct((rows, width), BF16),
            jax.ShapeDtypeStruct((rows, QW), BF16),
            jax.ShapeDtypeStruct((rows, cols), BF16),
            *four_shapes(work, width),
        ),
        scratch_shapes=[
            pltpu.VMEM((width, cols), BF16),
            pltpu.VMEM((QW, width), BF16),
            pltpu.VMEM((rows, cols), F32),
        ],
        cost_estimate=BESIDE,
        name="attention_forward",
    )(*pieces, w_qkv, w_out, cosine, sine, seg_col, seg_row)


def attention_backward(
    pieces, w_out, w_qkv, n_one, head_out, turned, cosine, sine, seg_col, seg_row, core, blocks
):
    work, width = pieces[0].shape
    rows = work * blocks
    cols = QW + 2 * HEAD_DIM
    share, members, each = w_qkv.shape[:3]
    heads = w_out.shape[1]

    def kernel(*refs):
        go_ref, gq_ref, n_ref, a_ref, r_ref, c_ref, s_ref, sc_ref, sr_ref = refs[5:14]
        core_ref, k_ref, mine_ref, other_ref = refs[14:18]
        d_ref, o_ref, h_ref, wq, wo = refs[23:]
        four_load(refs[:5], d_ref)
        in_order(go_ref, wo)
        h_ref[...] = dot_nt(d_ref[...], wo[...]).astype(BF16)
        in_order(gq_ref, wq)
        for b in range(blocks):
            at = slice(b * work, (b + 1) * work)
            c, s = c_ref[at], -s_ref[at]
            q = stack_heads(r_ref[at, :QW])
            k = r_ref[at, QW : QW + HEAD_DIM]
            v = r_ref[at, QW + HEAD_DIM :]
            d = stack_heads(h_ref[at])
            prob = probabilities(q, k, sc_ref[b], sr_ref[b])
            d_prob = dot_nt(d, v)
            d_v = dot_tn(prob.astype(BF16), d)
            d_s = prob * (d_prob - jnp.sum(prob * d_prob, axis=-1, keepdims=True))
            d_s = d_s.astype(BF16)
            d_q = dot(d_s, k) * FACTOR
            d_k = dot_tn(d_s, q) * FACTOR
            for i in range(GROUP):
                part = rotate(d_q[i * work : (i + 1) * work], c, s)
                o_ref[at, i * HEAD_DIM : (i + 1) * HEAD_DIM] = part.astype(BF16)
            o_ref[at, QW : QW + HEAD_DIM] = rotate(d_k, c, s).astype(BF16)
            o_ref[at, QW + HEAD_DIM :] = d_v.astype(BF16)
        four_store(refs[18:23], dot_nt(o_ref[...], wq[...]).astype(BF16))
        step = share * each
        for m in range(members):
            grad = dot_tn(n_ref[:, m * step : (m + 1) * step], o_ref[...]).astype(BF16)
            for i in range(share):
                k_ref[i, m] = grad[i * each : (i + 1) * each]
        for m in range(heads):
            grad = dot_tn(a_ref[:, m * step : (m + 1) * step], d_ref[...]).astype(BF16)
            for core in range(2):
                for x in range(share // 2):
                    at = (2 * x + core) * each

                    @pl.when(core_ref[0] == core)
                    def _(x=x, at=at, m=m, grad=grad):
                        mine_ref[x, m] = grad[at : at + each]

                    @pl.when(core_ref[0] != core)
                    def _(x=x, at=at, m=m, grad=grad):
                        other_ref[x, m] = grad[at : at + each]

    return pl.pallas_call(
        kernel,
        out_shape=(
            jax.ShapeDtypeStruct((share, members, each, cols), BF16),
            jax.ShapeDtypeStruct((share // 2, heads, each, width), BF16),
            jax.ShapeDtypeStruct((share // 2, heads, each, width), BF16),
            *four_shapes(work, width),
        ),
        in_specs=[pl.BlockSpec(memory_space=pltpu.VMEM)] * 14 + [pl.BlockSpec(memory_space=pltpu.SMEM)],
        scratch_shapes=[
            pltpu.VMEM((rows, width), BF16),
            pltpu.VMEM((rows, cols), BF16),
            pltpu.VMEM((rows, QW), BF16),
            pltpu.VMEM((width, cols), BF16),
            pltpu.VMEM((QW, width), BF16),
        ],
        cost_estimate=BESIDE,
        name="attention_backward",
    )(*pieces, w_out, w_qkv, n_one, head_out, turned, cosine, sine, seg_col, seg_row, core)


def norm_back(grad_out, values_in, scale_rows, gain_row):
    scaled_grad = grad_out * gain_row
    grad_in = scale_rows * scaled_grad - values_in * scale_rows**3 * jnp.mean(
        scaled_grad * values_in, axis=-1, keepdims=True
    )
    grad_gain = jnp.sum(grad_out * values_in * scale_rows, axis=0)
    return (grad_in, grad_gain)


def make(n):
    nh = n // 16
    nt = 4
    nz = 2 * nh
    nu = 2 * nz

    head_bits = n // KEY_VALUE_HEADS
    perm = []
    for src in range(n):
        a, rest = divmod(src, head_bits)
        h, xc = divmod(rest, 4)
        perm.append((src, h * 16 + a * 4 + xc))
    unperm = [(b, a) for a, b in perm]
    home = dict(unperm)
    cross = [(i, home[i ^ 16]) for i in range(n)]

    def shards(
        tokens,
        cotangent,
        send_row,
        recv_slot,
        segment,
        query_weight,
        key_weight,
        value_weight,
        out_weight,
        attn_gain,
        gate_weight,
        up_weight,
        down_weight,
        ffn_gain,
    ):
        width = tokens.shape[1]
        work = recv_slot.shape[0]
        slots = send_row.shape[0]
        cap = slots // n
        gw = attn_gain.shape[0]
        ffb = down_weight.shape[0]
        ff = 4 * ffb
        half = work // 2
        extra = -(-max(2 * gw, work) // 128) * 128

        slot = jnp.arange(slots, dtype=jnp.int32)
        row_of_slot = jnp.full((slots,), work, jnp.int32).at[recv_slot].set(slot[:work])
        slot_of_row = jnp.full((tokens.shape[0],), slots, jnp.int32)
        slot_of_row = slot_of_row.at[send_row].set(slot, mode="drop")
        o = Order(slot_of_row)
        sync = o.step

        def rows_at(rows, index):
            last = rows.shape[0] - 1
            found = rows.at[jnp.minimum(index, last)].get(mode="promise_in_bounds")
            return jnp.where((index <= last)[:, None], found, jnp.zeros((), BF16))

        def to_all(rows):
            return lax.all_to_all(rows, ALL, split_axis=0, concat_axis=0, tiled=True)

        gains = jnp.concatenate([attn_gain, ffn_gain])
        ext = jnp.zeros((cap, extra), BF16)
        ext = ext.at[0, : 2 * gw].set(gains).at[1, :work].set(segment.astype(BF16))
        ext = jnp.broadcast_to(ext[None], (n, cap, extra)).reshape(slots, extra)
        out_rows = rows_at(tokens, send_row)
        out_rows = jnp.concatenate([out_rows, ext], axis=1)

        heads = jnp.concatenate(
            [
                query_weight.reshape(gw, nt, QW),
                key_weight.reshape(gw, nt, HEAD_DIM),
                value_weight.reshape(gw, nt, HEAD_DIM),
            ],
            axis=2,
        )
        heads = jnp.transpose(heads, (1, 0, 2))
        heads = lax.all_to_all(heads, FOUR, split_axis=0, concat_axis=0, tiled=True)
        perm_out = lax.ppermute(out_weight, ALL, perm)
        heads, perm_out, out_rows, cotangent, gate_weight, up_weight = sync(
            heads, perm_out, out_rows, cotangent, gate_weight, up_weight
        )
        heads = heads.reshape(nt * gw, -1)
        out_cots = rows_at(cotangent, send_row)
        gu = split_columns(gate_weight, up_weight, nu)
        if nh == 2:
            qkv_h = swap(heads, "h")
            heads, qkv_h, out_cots, gu, out_rows = sync(heads, qkv_h, out_cots, gu, out_rows)
            qkv_h = pair(heads, qkv_h, "h")
        else:
            out_cots, gu, out_rows = sync(out_cots, gu, out_rows)
            qkv_h = lax.all_gather(heads, "h", axis=0, tiled=False)
        come = to_all(out_rows)
        qkv_h = sync(qkv_h)
        w_qkv = lax.all_gather(qkv_h.reshape(nh * nt * gw, -1), ("x", "c"), axis=0, tiled=True)
        out_h = swap(perm_out, "h") if nh == 2 else perm_out
        come = sync(come)
        t_me = lax.axis_index(FOUR)

        rows_bf = jnp.take(come[:, :width], recv_slot, axis=0)
        ext = come[:, width:].reshape(n, cap, extra)
        gain_one = ext[:, 0, :gw].reshape(n * gw).astype(F32)
        gain_two = ext[:, 0, gw : 2 * gw].reshape(n * gw).astype(F32)
        work_rows = rows_bf.astype(F32)
        scale_one = lax.rsqrt(jnp.mean(work_rows * work_rows, axis=-1, keepdims=True) + epsilon)
        n_own = sync((work_rows * scale_one * gain_one).astype(BF16))

        row_l, row_y = swap(n_own, "l"), swap(n_own, "y")
        if nh == 2:
            out_h = pair(*sync(perm_out, out_h), "h")
        else:
            out_h = lax.all_gather(perm_out, "h", axis=0, tiled=False)
        out_h = sync(out_h)
        w_out = lax.all_gather(out_h.reshape(nh * gw, -1), ("x", "c"), axis=0, tiled=True)
        w_out = w_out.reshape(4, nh, gw, -1)
        ext = sync(ext)
        me = lax.axis_index(ALL)
        seg = jnp.take(ext[:, 1, :work], jnp.stack([me, me ^ 8, me ^ 4, me ^ 12]), axis=0)
        seg = seg.astype(F32)
        row_index = jnp.arange(work, dtype=jnp.int32)
        allowed = (seg[:, :, None] == seg[:, None, :]) & (
            row_index[None, None, :] <= row_index[None, :, None]
        )
        position = jnp.sum(allowed.astype(F32), axis=-1) - 1.0
        freq = rope_base ** (-(jnp.arange(HEAD_DIM // 2, dtype=F32) * 2.0) / HEAD_DIM)
        phase = position.reshape(-1)[:, None] * freq[None, :]
        cosine = jnp.concatenate([jnp.cos(phase)] * 2, axis=1)
        sine = jnp.concatenate([-jnp.sin(phase), jnp.sin(phase)], axis=1)
        seg_col, seg_row = seg[:, :, None], seg[:, None, :]
        row_l, row_y, sine, cosine, seg_col, seg_row = sync(
            row_l, row_y, sine, cosine, seg_col, seg_row
        )
        row_ly = swap(row_y[:half], "l"), swap(row_l[half:], "y")
        w_qkv = w_qkv.reshape(4, nh * nt, gw, -1)
        row_ly, w_qkv, out_cots = sync(row_ly, w_qkv, out_cots)
        come_cots = to_all(out_cots)
        n_one, head_out, turned, *part = attention_forward(
            (n_own, row_l, row_y, *row_ly), w_qkv, w_out, cosine, sine, seg_col, seg_row, nt
        )
        n_one, head_out, turned, part, gu = sync(n_one, head_out, turned, part, gu)

        def sum_four(part, first, second):
            p, bl, by, low, high = part
            low, high = swap(low, "l"), swap(high, "y")
            (low, high), beside = sync((low, high), first())
            by = lax.dynamic_update_slice(by, add(by[:half], low), (0, 0))
            bl = lax.dynamic_update_slice(bl, add(bl[half:], high), (half, 0))
            by, bl = sync(by, bl)
            by, bl = swap(by, "y"), swap(bl, "l")
            (by, bl), beside = sync((by, bl), second(beside))
            return p.astype(F32) + bl.astype(F32) + by.astype(F32), beside

        w_down = lax.all_gather(down_weight, ("x", "c"), axis=0, tiled=True)

        def beside_sum(gu):
            gu = lax.all_to_all(gu, GROUP_F, split_axis=0, concat_axis=0, tiled=True)
            return gu, w_down

        attn, (gu, w_down) = sum_four(part, lambda: sync(gu, come_cots)[0], beside_sum)
        grad_bf = jnp.take(come_cots, recv_slot, axis=0)
        w_gu = lax.all_gather(gu.reshape(nu * gw, -1), ("x", "c"), axis=0, tiled=True)
        w_gu = w_gu.reshape(4, nu, gw, -1)

        hidden = work_rows + attn
        scale_two = lax.rsqrt(jnp.mean(hidden * hidden, axis=-1, keepdims=True) + epsilon)
        n_own = (hidden * scale_two * gain_two).astype(BF16)
        both_z, both_y = [sync(jnp.concatenate([n_own, grad_bf], axis=0))], []

        done = {}

        def step(i):
            return feed_forward(both_z[i], both_y[i], w_gu, w_down)

        for i in range(1, nz):
            nxt, oth = shift(both_z[-1], nz), swap(both_z[-1], "y")
            if i == nz - 1:
                w_gu = sync(w_gu)
                nxt, oth, done[1], done[0] = sync(nxt, oth, step(1), step(0))
            else:
                nxt, oth = sync(nxt, oth)
            both_z.append(nxt)
            both_y.append(oth)

        last = swap(both_z[-1][:work], "y"), shift(both_y[-1][work:], nz)
        *last, done[2] = sync(*last, step(2))
        both_y.append(tuple(last))

        own, other = done[1][2], done[1][3]
        sent = swap(other[:work], "y"), shift(other[work:], nz)
        for i in range(3, nz):
            done[i] = step(i)
        *sent, done = sync(*sent, done)
        acc = lax.dynamic_update_slice(own, add(own[:work], sent[0]), (0, 0))
        other = done[2][3]
        other = lax.dynamic_update_slice(other, add(other[work:], sent[1]), (work, 0))
        acc, other = sync(acc, other)
        acc, sent = shift(acc, nz), swap(other, "y")
        done = [done[i] for i in range(nz)]
        acts, d_gus, own, other = ([d[k] for d in done] for k in range(4))
        two_y, cot_y = [*both_y[:-1], both_y[-1][0]], [*both_y[:-1], both_y[-1][1]]
        lefts = [r for i in range(nz) for r in (both_z[i], two_y[i])]
        g_gu = shared_gradient(lefts, d_gus, 4, gw)
        g_gu, acc, sent = sync(g_gu, acc, sent)
        g_gu = lax.psum_scatter(g_gu, ("x", "c"), scatter_dimension=0, tiled=True)
        for i in range(2, nz):
            acc = sync(add(own[i], sent, acc))
            if i == nz - 1:
                break
            acc, sent = shift(acc, nz), swap(other[i + 1], "y")
            if i == 2:
                acc, sent, g_down = sync(acc, sent, down_gradient(acts, both_z, cot_y))
                g_down = lax.psum_scatter(g_down, ("x", "c"), scatter_dimension=0, tiled=True)
            else:
                acc, sent = sync(acc, sent)
        acc, sent = sync(shift(acc, nz), swap(other[0], "y"))
        total = own[0].astype(F32) + sent.astype(F32) + acc.astype(F32)
        d_hidden, d_gain_two = norm_back(total[:work], hidden, scale_two, gain_two)
        d_own = (grad_bf.astype(F32) + d_hidden).astype(BF16)
        delta = (attn + total[work:]).astype(BF16)
        d_hidden, d_own, delta, g_gu = sync(d_hidden, d_own, delta, g_gu)

        row_l, row_y = swap(d_own, "l"), swap(d_own, "y")
        slot_delta = rows_at(delta, row_of_slot)
        g_gu = lax.all_to_all(
            g_gu.reshape(nu, gw, -1), GROUP_F, split_axis=0, concat_axis=0, tiled=True
        )
        row_l, row_y, slot_delta = sync(row_l, row_y, slot_delta)
        row_ly = sync(swap(row_y[:half], "l"), swap(row_l[half:], "y"))
        g_qkv, mine, other, *part = attention_backward(
            (d_own, row_l, row_y, *row_ly),
            w_out,
            w_qkv,
            n_one,
            head_out,
            turned,
            cosine,
            sine,
            seg_col,
            seg_row,
            lax.axis_index("c").astype(jnp.int32).reshape(1),
            nt,
        )
        g_qkv, mine, other, part = sync(g_qkv, mine, other, part)
        g_qkv = lax.psum_scatter(
            g_qkv.reshape(width, -1), ("x", "c"), scatter_dimension=0, tiled=True
        )
        other = swap(other, "c")
        g_down, g_gu = sync(g_down, g_gu)

        def add_h(blocks):
            if nh != 2:
                return lax.psum_scatter(blocks, "h", scatter_dimension=0, tiled=False)
            mine, other = pick(blocks, "h")
            return add(mine, swap(other, "h"))

        def beside_last(pair_c):
            mine, other = pick(add(*pair_c), "x")
            return mine, swap(other, "x"), join_columns(g_gu), add_h(g_qkv.reshape(nh, nt * gw, -1))

        d_n_one, (mine, other, (g_gate, g_up), g_qkv) = sum_four(
            part, lambda: (mine, other), beside_last
        )
        g_qkv = g_qkv.reshape(nt, gw, -1)
        g_out = add(mine, other)
        if nh == 2:
            g_out = pick(g_out, "h")
        else:
            g_out = (lax.psum_scatter(g_out, "h", scatter_dimension=0, tiled=False),)
        g_out = sync(g_out)
        own, to_l, to_y, to_ly = sync(
            *(lax.dynamic_index_in_dim(g_qkv, t_me ^ r, 0, False) for r in (0, 2, 1, 3))
        )
        to_l, to_y = swap(to_l, "l"), swap(to_y, "y")
        to_ly = lax.ppermute(to_ly, FOUR, [(i, 3 - i) for i in range(4)])
        g_out = tuple(lax.ppermute(p, ALL, to) for p, to in zip(g_out, (unperm, cross)))
        d_norm, d_gain_one = norm_back(d_n_one, work_rows, scale_one, gain_one)
        back = (d_norm + d_hidden).astype(BF16)

        d_gains = jnp.concatenate([d_gain_one.reshape(n, gw), d_gain_two.reshape(n, gw)], axis=1)
        high = d_gains.astype(BF16)
        low = (d_gains - high.astype(F32)).astype(BF16)
        pad = jnp.zeros((n, cap - 2, 2 * gw), BF16)
        d_gains = jnp.concatenate([high[:, None], low[:, None], pad], axis=1)
        d_gains = jnp.pad(d_gains, ((0, 0), (0, 0), (0, extra - 2 * gw))).reshape(slots, extra)
        slot_back = rows_at(back, row_of_slot)
        slot_back = jnp.concatenate([slot_back, slot_delta, d_gains], axis=1)
        slot_back, own, to_l, to_y, to_ly, g_out = sync(slot_back, own, to_l, to_y, to_ly, g_out)
        got = to_all(slot_back)
        g_qkv = pair(pair(own, to_y, "y"), pair(to_l, to_ly, "y"), "l").reshape(nt, gw, -1)
        g_qkv = jnp.transpose(g_qkv.astype(F32), (1, 0, 2))
        g_down = g_down.astype(F32)
        g_out = sum(p.astype(F32) for p in g_out)
        g_qkv, g_down, g_out = sync(g_qkv, g_down, g_out)
        got = sync(got)
        d_gains = got[:, 2 * width :].reshape(n, cap, extra)[:, :2, : 2 * gw]
        d_gains = jnp.sum(d_gains.astype(F32), axis=(0, 1))
        local = rows_at(got, o.token)
        input_grad = (cotangent.astype(F32) + local[:, :width].astype(F32)).astype(BF16)
        output = (tokens.astype(F32) + local[:, width : 2 * width].astype(F32)).astype(BF16)
        g_query = g_qkv[:, :, :QW].reshape(gw, -1)
        g_key = g_qkv[:, :, QW : QW + HEAD_DIM].reshape(gw, -1)
        g_value = g_qkv[:, :, QW + HEAD_DIM :].reshape(gw, -1)
        return (
            output,
            input_grad,
            g_query,
            g_key,
            g_value,
            g_out,
            d_gains[:gw],
            g_gate,
            g_up,
            g_down,
            d_gains[gw:],
        )

    return shards


def solution(mesh):
    n = mesh.devices.size
    grid = Mesh(mesh.devices.reshape(n // 16, 2, 2, 2, 2), ALL)
    two, one = P(ALL, None), P(ALL)
    return jax.shard_map(
        make(n),
        mesh=grid,
        in_specs=(two, two, one, one, one, two, two, two, two, one, two, two, two, one),
        out_specs=(two, two, two, two, two, two, one, two, two, two, one),
        check_vma=False,
    )
```

```python
import jax
import jax.numpy as jnp
from jax import lax
from jax.experimental import pallas as pl
from jax.experimental.pallas import tpu as pltpu
from jax.sharding import Mesh, PartitionSpec as P

QUERY_HEADS = 16
KEY_VALUE_HEADS = 4
HEAD_DIM = 128
GROUP = QUERY_HEADS // KEY_VALUE_HEADS

epsilon = 1e-05
rope_base = 10000.0

ALL = ("h", "l", "y", "x", "c")
FOUR = ("l", "y")
LINE = ("h", "l")
GROUP_F = ("h", "l", "y")
F32 = jnp.float32
BF16 = jnp.bfloat16


def dot(left, right):
    return jnp.dot(left, right, preferred_element_type=F32)


def dot_tn(left, right):
    return lax.dot_general(left, right, (((0,), (0,)), ((), ())), preferred_element_type=F32)


def dot_nt(left, right):
    return lax.dot_general(left, right, (((1,), (1,)), ((), ())), preferred_element_type=F32)


def swap(block, axis):
    return lax.ppermute(block, axis, [(0, 1), (1, 0)])


def shift(block, size):
    return lax.ppermute(block, LINE, [(i, (i + 1) % size) for i in range(size)])


def pair(block, other, axis):
    first = lax.axis_index(axis) == 0
    return jnp.stack([jnp.where(first, block, other), jnp.where(first, other, block)])


def pick(blocks, axis):
    i = lax.axis_index(axis)
    mine = lax.dynamic_index_in_dim(blocks, i, 0, False)
    return mine, lax.dynamic_index_in_dim(blocks, 1 - i, 0, False)


def add(*parts):
    return sum(p.astype(F32) for p in parts).astype(BF16)


class Order:
    def __init__(self, token):
        self.token = token

    def step(self, *values):
        values = lax.optimization_barrier((*values, self.token))
        self.token = values[-1]
        return values[:-1] if len(values) > 2 else values[0]


def lanes(w):
    main = w // 128 * 128
    gate = ((slice(0, main), slice(0, main)), (slice(main, w), slice(2 * main, main + w)))
    up = ((slice(0, main), slice(main, 2 * main)), (slice(main, w), slice(main + w, 2 * w)))
    return gate, up


def split_columns(gate, up, parts):
    rows, cols = gate.shape
    w = cols // parts

    def kernel(g_ref, u_ref, o_ref):
        for j in range(parts):
            for ref, places in zip((g_ref, u_ref), lanes(w)):
                for at, to in places:
                    o_ref[j, :, to] = ref[:, j * w + at.start : j * w + at.stop]

    return pl.pallas_call(
        kernel,
        out_shape=jax.ShapeDtypeStruct((parts, rows, 2 * w), BF16),
        name="split_columns",
    )(gate, up)


def join_columns(blocks):
    parts, rows, w = blocks.shape
    w = w // 2

    def kernel(b_ref, g_ref, u_ref):
        for j in range(parts):
            for ref, places in zip((g_ref, u_ref), lanes(w)):
                for at, to in places:
                    ref[:, j * w + at.start : j * w + at.stop] = b_ref[j, :, to].astype(F32)

    out = jax.ShapeDtypeStruct((rows, parts * w), F32)
    return pl.pallas_call(kernel, out_shape=(out, out), name="join_columns")(blocks)


BESIDE = pl.CostEstimate(flops=1, bytes_accessed=1, transcendentals=0)


def feed_forward(first, second, w_gu, w_down):
    work, width = first.shape[0] // 2, first.shape[1]
    w = w_down.shape[0]
    parts = second if isinstance(second, tuple) else (second,)

    def kernel(a_ref, *refs):
        b_refs = refs[: len(parts)]
        r_ref, d_ref, act_ref, dgu_ref, own_ref, other_ref, g_ref = refs[len(parts) :]
        in_order(r_ref, g_ref)
        rows = jnp.concatenate([a_ref[:work], b_refs[0][:work]], axis=0)
        cots = jnp.concatenate([a_ref[work:], b_refs[-1][-work:]], axis=0)
        pre = dot(rows, g_ref[...])
        d_act = dot_nt(cots, d_ref[...])
        for (at, g), (_, u) in zip(*lanes(w)):
            if at.start == at.stop:
                continue
            gate, up, d = pre[:, g], pre[:, u], d_act[:, at]
            sig = 1.0 / (1.0 + jnp.exp(-gate))
            silu = gate * sig
            act_ref[:, at] = (silu * up).astype(BF16)
            dgu_ref[:, g] = (d * up * (sig * (1.0 + gate * (1.0 - sig)))).astype(BF16)
            dgu_ref[:, u] = (d * silu).astype(BF16)
        back = dot_nt(dgu_ref[...], g_ref[...]).astype(BF16)
        own_ref[:work], other_ref[:work] = back[:work], back[work:]
        out = dot(act_ref[...], d_ref[...]).astype(BF16)
        own_ref[work:], other_ref[work:] = out[:work], out[work:]

    def shape(cols):
        return jax.ShapeDtypeStruct((2 * work, cols), BF16)

    return pl.pallas_call(
        kernel,
        out_shape=(shape(w), shape(2 * w), shape(width), shape(width)),
        scratch_shapes=[pltpu.VMEM((width, 2 * w), BF16)],
        cost_estimate=BESIDE,
        name="feed_forward",
    )(first, *parts, w_gu, w_down)


def shared_gradient(lefts, rights, share, rows):
    count, each = len(rights), len(lefts) // len(rights)
    height, width = rights[0].shape[0], lefts[0].shape[1]
    cols = rights[0].shape[1]
    each_step = max(1, 256 // (share * rows))
    step = share * rows * each_step

    def kernel(*refs):
        ins, o_ref = refs[:-1], refs[-1]
        total = None
        for i in range(count):
            left = [ins[i * each + j][...] for j in range(each)]
            left = left[0] if each == 1 else jnp.concatenate(left, axis=0)
            part = dot_tn(left, ins[count * each + i][...])
            total = part if total is None else total + part
        for m in range(each_step):
            for i in range(share):
                at = (m * share + i) * rows
                o_ref[i, m] = total[at : at + rows].astype(BF16)

    left = pl.BlockSpec((height // each, step), lambda i: (0, i))
    right = pl.BlockSpec((height, cols), lambda i: (0, 0))
    return pl.pallas_call(
        kernel,
        grid=(width // step,),
        in_specs=[left] * (count * each) + [right] * count,
        out_specs=pl.BlockSpec((share, each_step, rows, cols), lambda i: (0, i, 0, 0)),
        out_shape=jax.ShapeDtypeStruct((share, width // step * each_step, rows, cols), BF16),
        cost_estimate=BESIDE,
        name="shared_gradient",
    )(*lefts, *rights).reshape(width, cols)


def down_gradient(acts, firsts, seconds):
    count = len(acts)
    work, width = firsts[0].shape[0] // 2, firsts[0].shape[1]
    w = acts[0].shape[1]
    step = 256

    def kernel(*refs):
        ins, o_ref = refs[:-1], refs[-1]
        total = None
        for i in range(count):
            right = jnp.concatenate([ins[count + i][...], ins[2 * count + i][...]], axis=0)
            part = dot_tn(ins[i][...], right)
            total = part if total is None else total + part
        o_ref[...] = total.astype(BF16)

    left = pl.BlockSpec((2 * work, w), lambda i: (0, 0))
    rights = [
        pl.BlockSpec((work, step), lambda i, at=r.shape[0] // work - 1: (at, i))
        for r in (*firsts, *seconds)
    ]
    return pl.pallas_call(
        kernel,
        grid=(width // step,),
        in_specs=[left] * count + rights,
        out_specs=pl.BlockSpec((w, step), lambda i: (0, i)),
        out_shape=jax.ShapeDtypeStruct((w, width), BF16),
        cost_estimate=BESIDE,
        name="down_gradient",
    )(*acts, *firsts, *seconds)


QW = GROUP * HEAD_DIM
FACTOR = HEAD_DIM ** (-0.5)


def rotate(values, cosine, sine):
    return values * cosine + pltpu.roll(values, HEAD_DIM // 2, 1) * sine


def probabilities(q, k, seg_col, seg_row):
    work = k.shape[0]
    row = lax.broadcasted_iota(jnp.int32, (work, work), 0)
    col = lax.broadcasted_iota(jnp.int32, (work, work), 1)
    allowed = (seg_col == seg_row) & (col <= row)
    allowed = jnp.concatenate([allowed.astype(F32)] * GROUP, axis=0) > 0.5
    scores = jnp.where(allowed, dot_nt(q, k) * FACTOR, -1e30)
    exps = jnp.exp(scores - jnp.max(scores, axis=-1, keepdims=True))
    return exps / jnp.sum(exps, axis=-1, keepdims=True)


def stack_heads(values):
    return jnp.concatenate([values[:, i * HEAD_DIM : (i + 1) * HEAD_DIM] for i in range(GROUP)], axis=0)


def lay_heads(values):
    work = values.shape[0] // GROUP
    return jnp.concatenate([values[i * work : (i + 1) * work] for i in range(GROUP)], axis=1)


def in_order(from_ref, to_ref):
    share, members, rows = from_ref.shape[:3]
    for i in range(share):
        for m in range(members):
            at = (m * share + i) * rows
            to_ref[at : at + rows, :] = from_ref[i, m]


def four_shapes(work, width):
    full, half = (jax.ShapeDtypeStruct((r, width), BF16) for r in (work, work // 2))
    return (full, full, full, half, half)


def four_store(refs, values):
    at = 0
    for ref in refs:
        ref[...] = values[at : at + ref.shape[0]]
        at += ref.shape[0]


def four_load(refs, to_ref):
    at = 0
    for ref in refs:
        to_ref[at : at + ref.shape[0], :] = ref[...]
        at += ref.shape[0]


def attention_forward(pieces, w_qkv, w_out, cosine, sine, seg_col, seg_row, blocks):
    work, width = pieces[0].shape
    rows = work * blocks
    cols = QW + 2 * HEAD_DIM

    def kernel(*refs):
        gq_ref, go_ref, c_ref, s_ref, sc_ref, sr_ref, n_ref, o_ref, r_ref = refs[5:14]
        wq, wo, x_ref = refs[19:]
        four_load(refs[:5], n_ref)
        in_order(gq_ref, wq)
        x_ref[...] = dot(n_ref[...], wq[...])
        in_order(go_ref, wo)
        for b in range(blocks):
            at = slice(b * work, (b + 1) * work)
            c, s = c_ref[at], s_ref[at]
            heads = [rotate(x_ref[at, i * HEAD_DIM : (i + 1) * HEAD_DIM], c, s) for i in range(GROUP + 1)]
            q = jnp.concatenate(heads[:GROUP], axis=0).astype(BF16)
            k = heads[GROUP].astype(BF16)
            v = x_ref[at, QW + HEAD_DIM :].astype(BF16)
            prob = probabilities(q, k, sc_ref[b], sr_ref[b])
            o_ref[at] = lay_heads(dot(prob.astype(BF16), v)).astype(BF16)
            for i in range(GROUP):
                r_ref[at, i * HEAD_DIM : (i + 1) * HEAD_DIM] = heads[i].astype(BF16)
            r_ref[at, QW : QW + HEAD_DIM] = k
            r_ref[at, QW + HEAD_DIM :] = v
        four_store(refs[14:19], dot(o_ref[...], wo[...]).astype(BF16))

    return pl.pallas_call(
        kernel,
        out_shape=(
            jax.ShapeDtypeStruct((rows, width), BF16),
            jax.ShapeDtypeStruct((rows, QW), BF16),
            jax.ShapeDtypeStruct((rows, cols), BF16),
            *four_shapes(work, width),
        ),
        scratch_shapes=[
            pltpu.VMEM((width, cols), BF16),
            pltpu.VMEM((QW, width), BF16),
            pltpu.VMEM((rows, cols), F32),
        ],
        cost_estimate=BESIDE,
        name="attention_forward",
    )(*pieces, w_qkv, w_out, cosine, sine, seg_col, seg_row)


def attention_backward(
    pieces, w_out, w_qkv, n_one, head_out, turned, cosine, sine, seg_col, seg_row, core, blocks
):
    work, width = pieces[0].shape
    rows = work * blocks
    cols = QW + 2 * HEAD_DIM
    share, members, each = w_qkv.shape[:3]
    heads = w_out.shape[1]

    def kernel(*refs):
        go_ref, gq_ref, n_ref, a_ref, r_ref, c_ref, s_ref, sc_ref, sr_ref = refs[5:14]
        core_ref, k_ref, mine_ref, other_ref = refs[14:18]
        d_ref, o_ref, h_ref, wq, wo = refs[23:]
        four_load(refs[:5], d_ref)
        in_order(go_ref, wo)
        h_ref[...] = dot_nt(d_ref[...], wo[...]).astype(BF16)
        in_order(gq_ref, wq)
        for b in range(blocks):
            at = slice(b * work, (b + 1) * work)
            c, s = c_ref[at], -s_ref[at]
            q = stack_heads(r_ref[at, :QW])
            k = r_ref[at, QW : QW + HEAD_DIM]
            v = r_ref[at, QW + HEAD_DIM :]
            d = stack_heads(h_ref[at])
            prob = probabilities(q, k, sc_ref[b], sr_ref[b])
            d_prob = dot_nt(d, v)
            d_v = dot_tn(prob.astype(BF16), d)
            d_s = prob * (d_prob - jnp.sum(prob * d_prob, axis=-1, keepdims=True))
            d_s = d_s.astype(BF16)
            d_q = dot(d_s, k) * FACTOR
            d_k = dot_tn(d_s, q) * FACTOR
            for i in range(GROUP):
                part = rotate(d_q[i * work : (i + 1) * work], c, s)
                o_ref[at, i * HEAD_DIM : (i + 1) * HEAD_DIM] = part.astype(BF16)
            o_ref[at, QW : QW + HEAD_DIM] = rotate(d_k, c, s).astype(BF16)
            o_ref[at, QW + HEAD_DIM :] = d_v.astype(BF16)
        four_store(refs[18:23], dot_nt(o_ref[...], wq[...]).astype(BF16))
        step = share * each
        for m in range(members):
            grad = dot_tn(n_ref[:, m * step : (m + 1) * step], o_ref[...]).astype(BF16)
            for i in range(share):
                k_ref[i, m] = grad[i * each : (i + 1) * each]
        for m in range(heads):
            grad = dot_tn(a_ref[:, m * step : (m + 1) * step], d_ref[...]).astype(BF16)
            for core in range(2):
                for x in range(share // 2):
                    at = (2 * x + core) * each

                    @pl.when(core_ref[0] == core)
                    def _(x=x, at=at, m=m, grad=grad):
                        mine_ref[x, m] = grad[at : at + each]

                    @pl.when(core_ref[0] != core)
                    def _(x=x, at=at, m=m, grad=grad):
                        other_ref[x, m] = grad[at : at + each]

    return pl.pallas_call(
        kernel,
        out_shape=(
            jax.ShapeDtypeStruct((share, members, each, cols), BF16),
            jax.ShapeDtypeStruct((share // 2, heads, each, width), BF16),
            jax.ShapeDtypeStruct((share // 2, heads, each, width), BF16),
            *four_shapes(work, width),
        ),
        in_specs=[pl.BlockSpec(memory_space=pltpu.VMEM)] * 14 + [pl.BlockSpec(memory_space=pltpu.SMEM)],
        scratch_shapes=[
            pltpu.VMEM((rows, width), BF16),
            pltpu.VMEM((rows, cols), BF16),
            pltpu.VMEM((rows, QW), BF16),
            pltpu.VMEM((width, cols), BF16),
            pltpu.VMEM((QW, width), BF16),
        ],
        cost_estimate=BESIDE,
        name="attention_backward",
    )(*pieces, w_out, w_qkv, n_one, head_out, turned, cosine, sine, seg_col, seg_row, core)


def norm_back(grad_out, values_in, scale_rows, gain_row):
    scaled_grad = grad_out * gain_row
    grad_in = scale_rows * scaled_grad - values_in * scale_rows**3 * jnp.mean(
        scaled_grad * values_in, axis=-1, keepdims=True
    )
    grad_gain = jnp.sum(grad_out * values_in * scale_rows, axis=0)
    return (grad_in, grad_gain)


def make(n):
    nh = n // 16
    nt = 4
    nz = 2 * nh
    nu = 2 * nz

    head_bits = n // KEY_VALUE_HEADS
    perm = []
    for src in range(n):
        a, rest = divmod(src, head_bits)
        h, xc = divmod(rest, 4)
        perm.append((src, h * 16 + a * 4 + xc))
    unperm = [(b, a) for a, b in perm]
    home = dict(unperm)
    cross = [(i, home[i ^ 16]) for i in range(n)]

    def shards(
        tokens,
        cotangent,
        send_row,
        recv_slot,
        segment,
        query_weight,
        key_weight,
        value_weight,
        out_weight,
        attn_gain,
        gate_weight,
        up_weight,
        down_weight,
        ffn_gain,
    ):
        width = tokens.shape[1]
        work = recv_slot.shape[0]
        slots = send_row.shape[0]
        cap = slots // n
        gw = attn_gain.shape[0]
        ffb = down_weight.shape[0]
        ff = 4 * ffb
        half = work // 2
        extra = -(-max(2 * gw, work) // 128) * 128

        slot = jnp.arange(slots, dtype=jnp.int32)
        row_of_slot = jnp.full((slots,), work, jnp.int32).at[recv_slot].set(slot[:work])
        slot_of_row = jnp.full((tokens.shape[0],), slots, jnp.int32)
        slot_of_row = slot_of_row.at[send_row].set(slot, mode="drop")
        o = Order(slot_of_row)
        sync = o.step

        def rows_at(rows, index):
            last = rows.shape[0] - 1
            found = rows.at[jnp.minimum(index, last)].get(mode="promise_in_bounds")
            return jnp.where((index <= last)[:, None], found, jnp.zeros((), BF16))

        def to_all(rows):
            return lax.all_to_all(rows, ALL, split_axis=0, concat_axis=0, tiled=True)

        gains = jnp.concatenate([attn_gain, ffn_gain])
        ext = jnp.zeros((cap, extra), BF16)
        ext = ext.at[0, : 2 * gw].set(gains).at[1, :work].set(segment.astype(BF16))
        ext = jnp.broadcast_to(ext[None], (n, cap, extra)).reshape(slots, extra)
        out_rows = rows_at(tokens, send_row)
        out_rows = jnp.concatenate([out_rows, ext], axis=1)

        heads = jnp.concatenate(
            [
                query_weight.reshape(gw, nt, QW),
                key_weight.reshape(gw, nt, HEAD_DIM),
                value_weight.reshape(gw, nt, HEAD_DIM),
            ],
            axis=2,
        )
        heads = jnp.transpose(heads, (1, 0, 2))
        heads = lax.all_to_all(heads, FOUR, split_axis=0, concat_axis=0, tiled=True)
        perm_out = lax.ppermute(out_weight, ALL, perm)
        heads, perm_out, out_rows, cotangent, gate_weight, up_weight = sync(
            heads, perm_out, out_rows, cotangent, gate_weight, up_weight
        )
        heads = heads.reshape(nt * gw, -1)
        out_cots = rows_at(cotangent, send_row)
        gu = split_columns(gate_weight, up_weight, nu)
        if nh == 2:
            qkv_h = swap(heads, "h")
            heads, qkv_h, out_cots, gu, out_rows = sync(heads, qkv_h, out_cots, gu, out_rows)
            qkv_h = pair(heads, qkv_h, "h")
        else:
            out_cots, gu, out_rows = sync(out_cots, gu, out_rows)
            qkv_h = lax.all_gather(heads, "h", axis=0, tiled=False)
        come = to_all(out_rows)
        qkv_h = sync(qkv_h)
        w_qkv = lax.all_gather(qkv_h.reshape(nh * nt * gw, -1), ("x", "c"), axis=0, tiled=True)
        out_h = swap(perm_out, "h") if nh == 2 else perm_out
        come = sync(come)
        t_me = lax.axis_index(FOUR)

        rows_bf = jnp.take(come[:, :width], recv_slot, axis=0)
        ext = come[:, width:].reshape(n, cap, extra)
        gain_one = ext[:, 0, :gw].reshape(n * gw).astype(F32)
        gain_two = ext[:, 0, gw : 2 * gw].reshape(n * gw).astype(F32)
        work_rows = rows_bf.astype(F32)
        scale_one = lax.rsqrt(jnp.mean(work_rows * work_rows, axis=-1, keepdims=True) + epsilon)
        n_own = sync((work_rows * scale_one * gain_one).astype(BF16))

        row_l, row_y = swap(n_own, "l"), swap(n_own, "y")
        if nh == 2:
            out_h = pair(*sync(perm_out, out_h), "h")
        else:
            out_h = lax.all_gather(perm_out, "h", axis=0, tiled=False)
        out_h = sync(out_h)
        w_out = lax.all_gather(out_h.reshape(nh * gw, -1), ("x", "c"), axis=0, tiled=True)
        w_out = w_out.reshape(4, nh, gw, -1)
        ext = sync(ext)
        me = lax.axis_index(ALL)
        seg = jnp.take(ext[:, 1, :work], jnp.stack([me, me ^ 8, me ^ 4, me ^ 12]), axis=0)
        seg = seg.astype(F32)
        row_index = jnp.arange(work, dtype=jnp.int32)
        allowed = (seg[:, :, None] == seg[:, None, :]) & (
            row_index[None, None, :] <= row_index[None, :, None]
        )
        position = jnp.sum(allowed.astype(F32), axis=-1) - 1.0
        freq = rope_base ** (-(jnp.arange(HEAD_DIM // 2, dtype=F32) * 2.0) / HEAD_DIM)
        phase = position.reshape(-1)[:, None] * freq[None, :]
        cosine = jnp.concatenate([jnp.cos(phase)] * 2, axis=1)
        sine = jnp.concatenate([-jnp.sin(phase), jnp.sin(phase)], axis=1)
        seg_col, seg_row = seg[:, :, None], seg[:, None, :]
        row_l, row_y, sine, cosine, seg_col, seg_row = sync(
            row_l, row_y, sine, cosine, seg_col, seg_row
        )
        row_ly = swap(row_y[:half], "l"), swap(row_l[half:], "y")
        w_qkv = w_qkv.reshape(4, nh * nt, gw, -1)
        row_ly, w_qkv, out_cots = sync(row_ly, w_qkv, out_cots)
        come_cots = to_all(out_cots)
        n_one, head_out, turned, *part = attention_forward(
            (n_own, row_l, row_y, *row_ly), w_qkv, w_out, cosine, sine, seg_col, seg_row, nt
        )
        n_one, head_out, turned, part, gu = sync(n_one, head_out, turned, part, gu)

        def sum_four(part, first, second):
            p, bl, by, low, high = part
            low, high = swap(low, "l"), swap(high, "y")
            (low, high), beside = sync((low, high), first())
            by = lax.dynamic_update_slice(by, add(by[:half], low), (0, 0))
            bl = lax.dynamic_update_slice(bl, add(bl[half:], high), (half, 0))
            by, bl = sync(by, bl)
            by, bl = swap(by, "y"), swap(bl, "l")
            (by, bl), beside = sync((by, bl), second(beside))
            return p.astype(F32) + bl.astype(F32) + by.astype(F32), beside

        w_down = lax.all_gather(down_weight, ("x", "c"), axis=0, tiled=True)

        def beside_sum(gu):
            gu = lax.all_to_all(gu, GROUP_F, split_axis=0, concat_axis=0, tiled=True)
            return gu, w_down

        attn, (gu, w_down) = sum_four(part, lambda: sync(gu, come_cots)[0], beside_sum)
        grad_bf = jnp.take(come_cots, recv_slot, axis=0)
        w_gu = lax.all_gather(gu.reshape(nu * gw, -1), ("x", "c"), axis=0, tiled=True)
        w_gu = w_gu.reshape(4, nu, gw, -1)

        hidden = work_rows + attn
        scale_two = lax.rsqrt(jnp.mean(hidden * hidden, axis=-1, keepdims=True) + epsilon)
        n_own = (hidden * scale_two * gain_two).astype(BF16)
        both_z, both_y = [sync(jnp.concatenate([n_own, grad_bf], axis=0))], []

        done = {}

        def step(i):
            return feed_forward(both_z[i], both_y[i], w_gu, w_down)

        for i in range(1, nz):
            nxt, oth = shift(both_z[-1], nz), swap(both_z[-1], "y")
            if i == nz - 1:
                w_gu = sync(w_gu)
                nxt, oth, done[1], done[0] = sync(nxt, oth, step(1), step(0))
            else:
                nxt, oth = sync(nxt, oth)
            both_z.append(nxt)
            both_y.append(oth)

        last = swap(both_z[-1][:work], "y"), shift(both_y[-1][work:], nz)
        *last, done[2] = sync(*last, step(2))
        both_y.append(tuple(last))

        own, other = done[1][2], done[1][3]
        sent = swap(other[:work], "y"), shift(other[work:], nz)
        for i in range(3, nz):
            done[i] = step(i)
        *sent, done = sync(*sent, done)
        acc = lax.dynamic_update_slice(own, add(own[:work], sent[0]), (0, 0))
        other = done[2][3]
        other = lax.dynamic_update_slice(other, add(other[work:], sent[1]), (work, 0))
        acc, other = sync(acc, other)
        acc, sent = shift(acc, nz), swap(other, "y")
        done = [done[i] for i in range(nz)]
        acts, d_gus, own, other = ([d[k] for d in done] for k in range(4))
        two_y, cot_y = [*both_y[:-1], both_y[-1][0]], [*both_y[:-1], both_y[-1][1]]
        lefts = [r for i in range(nz) for r in (both_z[i], two_y[i])]
        g_gu = shared_gradient(lefts, d_gus, 4, gw)
        g_gu, acc, sent = sync(g_gu, acc, sent)
        g_gu = lax.psum_scatter(g_gu, ("x", "c"), scatter_dimension=0, tiled=True)
        for i in range(2, nz):
            acc = sync(add(own[i], sent, acc))
            if i == nz - 1:
                break
            acc, sent = shift(acc, nz), swap(other[i + 1], "y")
            if i == 2:
                acc, sent, g_down = sync(acc, sent, down_gradient(acts, both_z, cot_y))
                g_down = lax.psum_scatter(g_down, ("x", "c"), scatter_dimension=0, tiled=True)
            else:
                acc, sent = sync(acc, sent)
        acc, sent = sync(shift(acc, nz), swap(other[0], "y"))
        total = own[0].astype(F32) + sent.astype(F32) + acc.astype(F32)
        d_hidden, d_gain_two = norm_back(total[:work], hidden, scale_two, gain_two)
        d_own = (grad_bf.astype(F32) + d_hidden).astype(BF16)
        delta = (attn + total[work:]).astype(BF16)
        d_hidden, d_own, delta, g_gu = sync(d_hidden, d_own, delta, g_gu)

        row_l, row_y = swap(d_own, "l"), swap(d_own, "y")
        slot_delta = rows_at(delta, row_of_slot)
        g_gu = lax.all_to_all(
            g_gu.reshape(nu, gw, -1), GROUP_F, split_axis=0, concat_axis=0, tiled=True
        )
        row_l, row_y, slot_delta = sync(row_l, row_y, slot_delta)
        row_ly = sync(swap(row_y[:half], "l"), swap(row_l[half:], "y"))
        g_qkv, mine, other, *part = attention_backward(
            (d_own, row_l, row_y, *row_ly),
            w_out,
            w_qkv,
            n_one,
            head_out,
            turned,
            cosine,
            sine,
            seg_col,
            seg_row,
            lax.axis_index("c").astype(jnp.int32).reshape(1),
            nt,
        )
        g_qkv, mine, other, part = sync(g_qkv, mine, other, part)
        g_qkv = lax.psum_scatter(
            g_qkv.reshape(width, -1), ("x", "c"), scatter_dimension=0, tiled=True
        )
        other = swap(other, "c")
        g_down, g_gu = sync(g_down, g_gu)

        def add_h(blocks):
            if nh != 2:
                return lax.psum_scatter(blocks, "h", scatter_dimension=0, tiled=False)
            mine, other = pick(blocks, "h")
            return add(mine, swap(other, "h"))

        def beside_last(pair_c):
            mine, other = pick(add(*pair_c), "x")
            return mine, swap(other, "x"), join_columns(g_gu), add_h(g_qkv.reshape(nh, nt * gw, -1))

        d_n_one, (mine, other, (g_gate, g_up), g_qkv) = sum_four(
            part, lambda: (mine, other), beside_last
        )
        d_norm, d_gain_one = norm_back(d_n_one, work_rows, scale_one, gain_one)
        back = (d_norm + d_hidden).astype(BF16)

        d_gains = jnp.concatenate([d_gain_one.reshape(n, gw), d_gain_two.reshape(n, gw)], axis=1)
        high = d_gains.astype(BF16)
        low = (d_gains - high.astype(F32)).astype(BF16)
        pad = jnp.zeros((n, cap - 2, 2 * gw), BF16)
        d_gains = jnp.concatenate([high[:, None], low[:, None], pad], axis=1)
        d_gains = jnp.pad(d_gains, ((0, 0), (0, 0), (0, extra - 2 * gw))).reshape(slots, extra)
        slot_back = rows_at(back, row_of_slot)
        slot_back = jnp.concatenate([slot_back, slot_delta, d_gains], axis=1)
        slot_back, g_qkv, mine, other = sync(slot_back, g_qkv, mine, other)
        got = to_all(slot_back)
        g_qkv = g_qkv.reshape(nt, gw, -1)
        g_out = add(mine, other)
        if nh == 2:
            g_out = pick(g_out, "h")
        else:
            g_out = (lax.psum_scatter(g_out, "h", scatter_dimension=0, tiled=False),)
        g_out = sync(g_out)
        own, to_l, to_y, to_ly = sync(
            *(lax.dynamic_index_in_dim(g_qkv, t_me ^ r, 0, False) for r in (0, 2, 1, 3))
        )
        to_l, to_y = swap(to_l, "l"), swap(to_y, "y")
        to_ly = lax.ppermute(to_ly, FOUR, [(i, 3 - i) for i in range(4)])
        g_out = tuple(lax.ppermute(p, ALL, to) for p, to in zip(g_out, (unperm, cross)))
        g_down = g_down.astype(F32)
        g_down, got = sync(g_down, got)
        d_gains = got[:, 2 * width :].reshape(n, cap, extra)[:, :2, : 2 * gw]
        d_gains = jnp.sum(d_gains.astype(F32), axis=(0, 1))
        local = rows_at(got, o.token)
        input_grad = (cotangent.astype(F32) + local[:, :width].astype(F32)).astype(BF16)
        output = (tokens.astype(F32) + local[:, width : 2 * width].astype(F32)).astype(BF16)
        own, to_l, to_y, to_ly, g_out, output, input_grad = sync(
            own, to_l, to_y, to_ly, g_out, output, input_grad
        )
        g_qkv = pair(pair(own, to_y, "y"), pair(to_l, to_ly, "y"), "l").reshape(nt, gw, -1)
        g_qkv = jnp.transpose(g_qkv.astype(F32), (1, 0, 2))
        g_out = sum(p.astype(F32) for p in g_out)
        g_query = g_qkv[:, :, :QW].reshape(gw, -1)
        g_key = g_qkv[:, :, QW : QW + HEAD_DIM].reshape(gw, -1)
        g_value = g_qkv[:, :, QW + HEAD_DIM :].reshape(gw, -1)
        return (
            output,
            input_grad,
            g_query,
            g_key,
            g_value,
            g_out,
            d_gains[:gw],
            g_gate,
            g_up,
            g_down,
            d_gains[gw:],
        )

    return shards


def solution(mesh):
    n = mesh.devices.size
    grid = Mesh(mesh.devices.reshape(n // 16, 2, 2, 2, 2), ALL)
    two, one = P(ALL, None), P(ALL)
    return jax.shard_map(
        make(n),
        mesh=grid,
        in_specs=(two, two, one, one, one, two, two, two, two, one, two, two, two, one),
        out_specs=(two, two, two, two, two, two, one, two, two, two, one),
        check_vma=False,
    )
```

```python
import jax
import jax.numpy as jnp
from jax import lax
from jax.experimental import pallas as pl
from jax.experimental.pallas import tpu as pltpu
from jax.sharding import Mesh, PartitionSpec as P

QUERY_HEADS = 16
KEY_VALUE_HEADS = 4
HEAD_DIM = 128
GROUP = QUERY_HEADS // KEY_VALUE_HEADS

epsilon = 1e-05
rope_base = 10000.0

ALL = ("h", "l", "y", "x", "c")
FOUR = ("l", "y")
LINE = ("h", "l")
GROUP_F = ("h", "l", "y")
F32 = jnp.float32
BF16 = jnp.bfloat16


def dot(left, right):
    return jnp.dot(left, right, preferred_element_type=F32)


def dot_tn(left, right):
    return lax.dot_general(left, right, (((0,), (0,)), ((), ())), preferred_element_type=F32)


def dot_nt(left, right):
    return lax.dot_general(left, right, (((1,), (1,)), ((), ())), preferred_element_type=F32)


def swap(block, axis):
    return lax.ppermute(block, axis, [(0, 1), (1, 0)])


def shift(block, size):
    return lax.ppermute(block, LINE, [(i, (i + 1) % size) for i in range(size)])


def pair(block, other, axis):
    first = lax.axis_index(axis) == 0
    return jnp.stack([jnp.where(first, block, other), jnp.where(first, other, block)])


def pick(blocks, axis):
    i = lax.axis_index(axis)
    mine = lax.dynamic_index_in_dim(blocks, i, 0, False)
    return mine, lax.dynamic_index_in_dim(blocks, 1 - i, 0, False)


def add(*parts):
    return sum(p.astype(F32) for p in parts).astype(BF16)


class Order:
    def __init__(self, token):
        self.token = token

    def step(self, *values):
        values = lax.optimization_barrier((*values, self.token))
        self.token = values[-1]
        return values[:-1] if len(values) > 2 else values[0]


def lanes(w):
    main = w // 128 * 128
    gate = ((slice(0, main), slice(0, main)), (slice(main, w), slice(2 * main, main + w)))
    up = ((slice(0, main), slice(main, 2 * main)), (slice(main, w), slice(main + w, 2 * w)))
    return gate, up


def split_columns(gate, up, parts):
    rows, cols = gate.shape
    w = cols // parts

    def kernel(g_ref, u_ref, o_ref):
        for j in range(parts):
            for ref, places in zip((g_ref, u_ref), lanes(w)):
                for at, to in places:
                    o_ref[j, :, to] = ref[:, j * w + at.start : j * w + at.stop]

    return pl.pallas_call(
        kernel,
        out_shape=jax.ShapeDtypeStruct((parts, rows, 2 * w), BF16),
        name="split_columns",
    )(gate, up)


def join_columns(blocks):
    parts, rows, w = blocks.shape
    w = w // 2

    def kernel(b_ref, g_ref, u_ref):
        for j in range(parts):
            for ref, places in zip((g_ref, u_ref), lanes(w)):
                for at, to in places:
                    ref[:, j * w + at.start : j * w + at.stop] = b_ref[j, :, to].astype(F32)

    out = jax.ShapeDtypeStruct((rows, parts * w), F32)
    return pl.pallas_call(kernel, out_shape=(out, out), name="join_columns")(blocks)


BESIDE = pl.CostEstimate(flops=1, bytes_accessed=1, transcendentals=0)


def feed_forward(first, second, w_gu, w_down):
    work, width = first.shape[0] // 2, first.shape[1]
    w = w_down.shape[0]
    parts = second if isinstance(second, tuple) else (second,)

    def kernel(a_ref, *refs):
        b_refs = refs[: len(parts)]
        r_ref, d_ref, act_ref, dgu_ref, own_ref, other_ref, g_ref = refs[len(parts) :]
        in_order(r_ref, g_ref)
        rows = jnp.concatenate([a_ref[:work], b_refs[0][:work]], axis=0)
        cots = jnp.concatenate([a_ref[work:], b_refs[-1][-work:]], axis=0)
        pre = dot(rows, g_ref[...])
        d_act = dot_nt(cots, d_ref[...])
        for (at, g), (_, u) in zip(*lanes(w)):
            if at.start == at.stop:
                continue
            gate, up, d = pre[:, g], pre[:, u], d_act[:, at]
            sig = 1.0 / (1.0 + jnp.exp(-gate))
            silu = gate * sig
            act_ref[:, at] = (silu * up).astype(BF16)
            dgu_ref[:, g] = (d * up * (sig * (1.0 + gate * (1.0 - sig)))).astype(BF16)
            dgu_ref[:, u] = (d * silu).astype(BF16)
        back = dot_nt(dgu_ref[...], g_ref[...]).astype(BF16)
        own_ref[:work], other_ref[:work] = back[:work], back[work:]
        out = dot(act_ref[...], d_ref[...]).astype(BF16)
        own_ref[work:], other_ref[work:] = out[:work], out[work:]

    def shape(cols):
        return jax.ShapeDtypeStruct((2 * work, cols), BF16)

    return pl.pallas_call(
        kernel,
        out_shape=(shape(w), shape(2 * w), shape(width), shape(width)),
        scratch_shapes=[pltpu.VMEM((width, 2 * w), BF16)],
        cost_estimate=BESIDE,
        name="feed_forward",
    )(first, *parts, w_gu, w_down)


def shared_gradient(lefts, rights, share, rows):
    count, each = len(rights), len(lefts) // len(rights)
    height, width = rights[0].shape[0], lefts[0].shape[1]
    cols = rights[0].shape[1]
    each_step = max(1, 256 // (share * rows))
    step = share * rows * each_step

    def kernel(*refs):
        ins, o_ref = refs[:-1], refs[-1]
        total = None
        for i in range(count):
            left = [ins[i * each + j][...] for j in range(each)]
            left = left[0] if each == 1 else jnp.concatenate(left, axis=0)
            part = dot_tn(left, ins[count * each + i][...])
            total = part if total is None else total + part
        for m in range(each_step):
            for i in range(share):
                at = (m * share + i) * rows
                o_ref[i, m] = total[at : at + rows].astype(BF16)

    left = pl.BlockSpec((height // each, step), lambda i: (0, i))
    right = pl.BlockSpec((height, cols), lambda i: (0, 0))
    return pl.pallas_call(
        kernel,
        grid=(width // step,),
        in_specs=[left] * (count * each) + [right] * count,
        out_specs=pl.BlockSpec((share, each_step, rows, cols), lambda i: (0, i, 0, 0)),
        out_shape=jax.ShapeDtypeStruct((share, width // step * each_step, rows, cols), BF16),
        cost_estimate=BESIDE,
        name="shared_gradient",
    )(*lefts, *rights).reshape(width, cols)


def down_gradient(acts, firsts, seconds):
    count = len(acts)
    work, width = firsts[0].shape[0] // 2, firsts[0].shape[1]
    w = acts[0].shape[1]
    step = 256

    def kernel(*refs):
        ins, o_ref = refs[:-1], refs[-1]
        total = None
        for i in range(count):
            right = jnp.concatenate([ins[count + i][...], ins[2 * count + i][...]], axis=0)
            part = dot_tn(ins[i][...], right)
            total = part if total is None else total + part
        o_ref[...] = total.astype(BF16)

    left = pl.BlockSpec((2 * work, w), lambda i: (0, 0))
    rights = [
        pl.BlockSpec((work, step), lambda i, at=r.shape[0] // work - 1: (at, i))
        for r in (*firsts, *seconds)
    ]
    return pl.pallas_call(
        kernel,
        grid=(width // step,),
        in_specs=[left] * count + rights,
        out_specs=pl.BlockSpec((w, step), lambda i: (0, i)),
        out_shape=jax.ShapeDtypeStruct((w, width), BF16),
        cost_estimate=BESIDE,
        name="down_gradient",
    )(*acts, *firsts, *seconds)


QW = GROUP * HEAD_DIM
FACTOR = HEAD_DIM ** (-0.5)


def rotate(values, cosine, sine):
    return values * cosine + pltpu.roll(values, HEAD_DIM // 2, 1) * sine


def probabilities(q, k, seg_col, seg_row):
    work = k.shape[0]
    row = lax.broadcasted_iota(jnp.int32, (work, work), 0)
    col = lax.broadcasted_iota(jnp.int32, (work, work), 1)
    allowed = (seg_col == seg_row) & (col <= row)
    allowed = jnp.concatenate([allowed.astype(F32)] * GROUP, axis=0) > 0.5
    scores = jnp.where(allowed, dot_nt(q, k) * FACTOR, -1e30)
    exps = jnp.exp(scores - jnp.max(scores, axis=-1, keepdims=True))
    return exps / jnp.sum(exps, axis=-1, keepdims=True)


def stack_heads(values):
    return jnp.concatenate([values[:, i * HEAD_DIM : (i + 1) * HEAD_DIM] for i in range(GROUP)], axis=0)


def lay_heads(values):
    work = values.shape[0] // GROUP
    return jnp.concatenate([values[i * work : (i + 1) * work] for i in range(GROUP)], axis=1)


def in_order(from_ref, to_ref):
    share, members, rows = from_ref.shape[:3]
    for i in range(share):
        for m in range(members):
            at = (m * share + i) * rows
            to_ref[at : at + rows, :] = from_ref[i, m]


def four_shapes(work, width):
    full, half = (jax.ShapeDtypeStruct((r, width), BF16) for r in (work, work // 2))
    return (full, full, full, half, half)


def four_store(refs, values):
    at = 0
    for ref in refs:
        ref[...] = values[at : at + ref.shape[0]]
        at += ref.shape[0]


def four_load(refs, to_ref):
    at = 0
    for ref in refs:
        to_ref[at : at + ref.shape[0], :] = ref[...]
        at += ref.shape[0]


def attention_forward(pieces, w_qkv, w_out, cosine, sine, seg_col, seg_row, blocks):
    work, width = pieces[0].shape
    rows = work * blocks
    cols = QW + 2 * HEAD_DIM

    def kernel(*refs):
        gq_ref, go_ref, c_ref, s_ref, sc_ref, sr_ref, n_ref, o_ref, r_ref = refs[5:14]
        wq, wo, x_ref = refs[19:]
        four_load(refs[:5], n_ref)
        in_order(gq_ref, wq)
        x_ref[...] = dot(n_ref[...], wq[...])
        in_order(go_ref, wo)
        for b in range(blocks):
            at = slice(b * work, (b + 1) * work)
            c, s = c_ref[at], s_ref[at]
            heads = [rotate(x_ref[at, i * HEAD_DIM : (i + 1) * HEAD_DIM], c, s) for i in range(GROUP + 1)]
            q = jnp.concatenate(heads[:GROUP], axis=0).astype(BF16)
            k = heads[GROUP].astype(BF16)
            v = x_ref[at, QW + HEAD_DIM :].astype(BF16)
            prob = probabilities(q, k, sc_ref[b], sr_ref[b])
            o_ref[at] = lay_heads(dot(prob.astype(BF16), v)).astype(BF16)
            for i in range(GROUP):
                r_ref[at, i * HEAD_DIM : (i + 1) * HEAD_DIM] = heads[i].astype(BF16)
            r_ref[at, QW : QW + HEAD_DIM] = k
            r_ref[at, QW + HEAD_DIM :] = v
        four_store(refs[14:19], dot(o_ref[...], wo[...]).astype(BF16))

    return pl.pallas_call(
        kernel,
        out_shape=(
            jax.ShapeDtypeStruct((rows, width), BF16),
            jax.ShapeDtypeStruct((rows, QW), BF16),
            jax.ShapeDtypeStruct((rows, cols), BF16),
            *four_shapes(work, width),
        ),
        scratch_shapes=[
            pltpu.VMEM((width, cols), BF16),
            pltpu.VMEM((QW, width), BF16),
            pltpu.VMEM((rows, cols), F32),
        ],
        cost_estimate=BESIDE,
        name="attention_forward",
    )(*pieces, w_qkv, w_out, cosine, sine, seg_col, seg_row)


def attention_backward(
    pieces, w_out, w_qkv, n_one, head_out, turned, cosine, sine, seg_col, seg_row, core, blocks
):
    work, width = pieces[0].shape
    rows = work * blocks
    cols = QW + 2 * HEAD_DIM
    share, members, each = w_qkv.shape[:3]
    heads = w_out.shape[1]

    def kernel(*refs):
        go_ref, gq_ref, n_ref, a_ref, r_ref, c_ref, s_ref, sc_ref, sr_ref = refs[5:14]
        core_ref, k_ref, mine_ref, other_ref = refs[14:18]
        d_ref, o_ref, h_ref, wq, wo = refs[23:]
        four_load(refs[:5], d_ref)
        in_order(go_ref, wo)
        h_ref[...] = dot_nt(d_ref[...], wo[...]).astype(BF16)
        in_order(gq_ref, wq)
        for b in range(blocks):
            at = slice(b * work, (b + 1) * work)
            c, s = c_ref[at], -s_ref[at]
            q = stack_heads(r_ref[at, :QW])
            k = r_ref[at, QW : QW + HEAD_DIM]
            v = r_ref[at, QW + HEAD_DIM :]
            d = stack_heads(h_ref[at])
            prob = probabilities(q, k, sc_ref[b], sr_ref[b])
            d_prob = dot_nt(d, v)
            d_v = dot_tn(prob.astype(BF16), d)
            d_s = prob * (d_prob - jnp.sum(prob * d_prob, axis=-1, keepdims=True))
            d_s = d_s.astype(BF16)
            d_q = dot(d_s, k) * FACTOR
            d_k = dot_tn(d_s, q) * FACTOR
            for i in range(GROUP):
                part = rotate(d_q[i * work : (i + 1) * work], c, s)
                o_ref[at, i * HEAD_DIM : (i + 1) * HEAD_DIM] = part.astype(BF16)
            o_ref[at, QW : QW + HEAD_DIM] = rotate(d_k, c, s).astype(BF16)
            o_ref[at, QW + HEAD_DIM :] = d_v.astype(BF16)
        four_store(refs[18:23], dot_nt(o_ref[...], wq[...]).astype(BF16))
        step = share * each
        for m in range(members):
            grad = dot_tn(n_ref[:, m * step : (m + 1) * step], o_ref[...]).astype(BF16)
            for i in range(share):
                k_ref[i, m] = grad[i * each : (i + 1) * each]
        for m in range(heads):
            grad = dot_tn(a_ref[:, m * step : (m + 1) * step], d_ref[...]).astype(BF16)
            for core in range(2):
                for x in range(share // 2):
                    at = (2 * x + core) * each

                    @pl.when(core_ref[0] == core)
                    def _(x=x, at=at, m=m, grad=grad):
                        mine_ref[x, m] = grad[at : at + each]

                    @pl.when(core_ref[0] != core)
                    def _(x=x, at=at, m=m, grad=grad):
                        other_ref[x, m] = grad[at : at + each]

    return pl.pallas_call(
        kernel,
        out_shape=(
            jax.ShapeDtypeStruct((share, members, each, cols), BF16),
            jax.ShapeDtypeStruct((share // 2, heads, each, width), BF16),
            jax.ShapeDtypeStruct((share // 2, heads, each, width), BF16),
            *four_shapes(work, width),
        ),
        in_specs=[pl.BlockSpec(memory_space=pltpu.VMEM)] * 14 + [pl.BlockSpec(memory_space=pltpu.SMEM)],
        scratch_shapes=[
            pltpu.VMEM((rows, width), BF16),
            pltpu.VMEM((rows, cols), BF16),
            pltpu.VMEM((rows, QW), BF16),
            pltpu.VMEM((width, cols), BF16),
            pltpu.VMEM((QW, width), BF16),
        ],
        cost_estimate=BESIDE,
        name="attention_backward",
    )(*pieces, w_out, w_qkv, n_one, head_out, turned, cosine, sine, seg_col, seg_row, core)


def norm_back(grad_out, values_in, scale_rows, gain_row):
    scaled_grad = grad_out * gain_row
    grad_in = scale_rows * scaled_grad - values_in * scale_rows**3 * jnp.mean(
        scaled_grad * values_in, axis=-1, keepdims=True
    )
    grad_gain = jnp.sum(grad_out * values_in * scale_rows, axis=0)
    return (grad_in, grad_gain)


def make(n):
    nh = n // 16
    nt = 4
    nz = 2 * nh
    nu = 2 * nz

    head_bits = n // KEY_VALUE_HEADS
    perm = []
    for src in range(n):
        a, rest = divmod(src, head_bits)
        h, xc = divmod(rest, 4)
        perm.append((src, h * 16 + a * 4 + xc))
    unperm = [(b, a) for a, b in perm]
    home = dict(unperm)
    cross = [(i, home[i ^ 16]) for i in range(n)]

    def shards(
        tokens,
        cotangent,
        send_row,
        recv_slot,
        segment,
        query_weight,
        key_weight,
        value_weight,
        out_weight,
        attn_gain,
        gate_weight,
        up_weight,
        down_weight,
        ffn_gain,
    ):
        width = tokens.shape[1]
        work = recv_slot.shape[0]
        slots = send_row.shape[0]
        cap = slots // n
        gw = attn_gain.shape[0]
        ffb = down_weight.shape[0]
        ff = 4 * ffb
        half = work // 2
        extra = -(-max(2 * gw, work) // 128) * 128

        slot = jnp.arange(slots, dtype=jnp.int32)
        row_of_slot = jnp.full((slots,), work, jnp.int32).at[recv_slot].set(slot[:work])
        slot_of_row = jnp.full((tokens.shape[0],), slots, jnp.int32)
        slot_of_row = slot_of_row.at[send_row].set(slot, mode="drop")
        o = Order(slot_of_row)
        sync = o.step

        def rows_at(rows, index):
            last = rows.shape[0] - 1
            found = rows.at[jnp.minimum(index, last)].get(mode="promise_in_bounds")
            return jnp.where((index <= last)[:, None], found, jnp.zeros((), BF16))

        def to_all(rows):
            return lax.all_to_all(rows, ALL, split_axis=0, concat_axis=0, tiled=True)

        gains = jnp.concatenate([attn_gain, ffn_gain])
        ext = jnp.zeros((cap, extra), BF16)
        ext = ext.at[0, : 2 * gw].set(gains).at[1, :work].set(segment.astype(BF16))
        ext = jnp.broadcast_to(ext[None], (n, cap, extra)).reshape(slots, extra)
        out_rows = rows_at(tokens, send_row)
        out_rows = jnp.concatenate([out_rows, ext], axis=1)

        heads = jnp.concatenate(
            [
                query_weight.reshape(gw, nt, QW),
                key_weight.reshape(gw, nt, HEAD_DIM),
                value_weight.reshape(gw, nt, HEAD_DIM),
            ],
            axis=2,
        )
        heads = jnp.transpose(heads, (1, 0, 2))
        heads = lax.all_to_all(heads, FOUR, split_axis=0, concat_axis=0, tiled=True)
        perm_out = lax.ppermute(out_weight, ALL, perm)
        heads, perm_out, out_rows, cotangent, gate_weight, up_weight = sync(
            heads, perm_out, out_rows, cotangent, gate_weight, up_weight
        )
        heads = heads.reshape(nt * gw, -1)
        out_cots = rows_at(cotangent, send_row)
        gu = split_columns(gate_weight, up_weight, nu)
        if nh == 2:
            qkv_h = swap(heads, "h")
            heads, qkv_h, out_cots, gu, out_rows = sync(heads, qkv_h, out_cots, gu, out_rows)
            qkv_h = pair(heads, qkv_h, "h")
        else:
            out_cots, gu, out_rows = sync(out_cots, gu, out_rows)
            qkv_h = lax.all_gather(heads, "h", axis=0, tiled=False)
        come = to_all(out_rows)
        qkv_h = sync(qkv_h)
        w_qkv = lax.all_gather(qkv_h.reshape(nh * nt * gw, -1), ("x", "c"), axis=0, tiled=True)
        out_h = swap(perm_out, "h") if nh == 2 else perm_out
        come = sync(come)
        t_me = lax.axis_index(FOUR)

        rows_bf = come.at[recv_slot].get(mode="promise_in_bounds")[:, :width]
        ext = come[:, width:].reshape(n, cap, extra)
        gain_one = ext[:, 0, :gw].reshape(n * gw).astype(F32)
        gain_two = ext[:, 0, gw : 2 * gw].reshape(n * gw).astype(F32)
        work_rows = rows_bf.astype(F32)
        scale_one = lax.rsqrt(jnp.mean(work_rows * work_rows, axis=-1, keepdims=True) + epsilon)
        n_own = sync((work_rows * scale_one * gain_one).astype(BF16))

        row_l, row_y = swap(n_own, "l"), swap(n_own, "y")
        if nh == 2:
            out_h = pair(*sync(perm_out, out_h), "h")
        else:
            out_h = lax.all_gather(perm_out, "h", axis=0, tiled=False)
        out_h = sync(out_h)
        w_out = lax.all_gather(out_h.reshape(nh * gw, -1), ("x", "c"), axis=0, tiled=True)
        w_out = w_out.reshape(4, nh, gw, -1)
        ext = sync(ext)
        me = lax.axis_index(ALL)
        seg = jnp.take(ext[:, 1, :work], jnp.stack([me, me ^ 8, me ^ 4, me ^ 12]), axis=0)
        seg = seg.astype(F32)
        row_index = jnp.arange(work, dtype=jnp.int32)
        allowed = (seg[:, :, None] == seg[:, None, :]) & (
            row_index[None, None, :] <= row_index[None, :, None]
        )
        position = jnp.sum(allowed.astype(F32), axis=-1) - 1.0
        freq = rope_base ** (-(jnp.arange(HEAD_DIM // 2, dtype=F32) * 2.0) / HEAD_DIM)
        phase = position.reshape(-1)[:, None] * freq[None, :]
        cosine = jnp.concatenate([jnp.cos(phase)] * 2, axis=1)
        sine = jnp.concatenate([-jnp.sin(phase), jnp.sin(phase)], axis=1)
        seg_col, seg_row = seg[:, :, None], seg[:, None, :]
        row_l, row_y, sine, cosine, seg_col, seg_row = sync(
            row_l, row_y, sine, cosine, seg_col, seg_row
        )
        row_ly = swap(row_y[:half], "l"), swap(row_l[half:], "y")
        w_qkv = w_qkv.reshape(4, nh * nt, gw, -1)
        row_ly, w_qkv, out_cots = sync(row_ly, w_qkv, out_cots)
        come_cots = to_all(out_cots)
        n_one, head_out, turned, *part = attention_forward(
            (n_own, row_l, row_y, *row_ly), w_qkv, w_out, cosine, sine, seg_col, seg_row, nt
        )
        n_one, head_out, turned, part, gu = sync(n_one, head_out, turned, part, gu)

        def sum_four(part, first, second):
            p, bl, by, low, high = part
            low, high = swap(low, "l"), swap(high, "y")
            (low, high), beside = sync((low, high), first())
            by = lax.dynamic_update_slice(by, add(by[:half], low), (0, 0))
            bl = lax.dynamic_update_slice(bl, add(bl[half:], high), (half, 0))
            by, bl = sync(by, bl)
            by, bl = swap(by, "y"), swap(bl, "l")
            (by, bl), beside = sync((by, bl), second(beside))
            return p.astype(F32) + bl.astype(F32) + by.astype(F32), beside

        w_down = lax.all_gather(down_weight, ("x", "c"), axis=0, tiled=True)

        def beside_sum(gu):
            gu = lax.all_to_all(gu, GROUP_F, split_axis=0, concat_axis=0, tiled=True)
            return gu, w_down

        attn, (gu, w_down) = sum_four(part, lambda: sync(gu, come_cots)[0], beside_sum)
        grad_bf = jnp.take(come_cots, recv_slot, axis=0)
        w_gu = lax.all_gather(gu.reshape(nu * gw, -1), ("x", "c"), axis=0, tiled=True)
        w_gu = w_gu.reshape(4, nu, gw, -1)

        hidden = work_rows + attn
        scale_two = lax.rsqrt(jnp.mean(hidden * hidden, axis=-1, keepdims=True) + epsilon)
        n_own = (hidden * scale_two * gain_two).astype(BF16)
        both_z, both_y = [sync(jnp.concatenate([n_own, grad_bf], axis=0))], []

        done = {}

        def step(i):
            return feed_forward(both_z[i], both_y[i], w_gu, w_down)

        for i in range(1, nz):
            nxt, oth = shift(both_z[-1], nz), swap(both_z[-1], "y")
            if i == nz - 1:
                w_gu = sync(w_gu)
                nxt, oth, done[1], done[0] = sync(nxt, oth, step(1), step(0))
            else:
                nxt, oth = sync(nxt, oth)
            both_z.append(nxt)
            both_y.append(oth)

        last = swap(both_z[-1][:work], "y"), shift(both_y[-1][work:], nz)
        *last, done[2] = sync(*last, step(2))
        both_y.append(tuple(last))

        own, other = done[1][2], done[1][3]
        sent = swap(other[:work], "y"), shift(other[work:], nz)
        for i in range(3, nz):
            done[i] = step(i)
        *sent, done = sync(*sent, done)
        acc = lax.dynamic_update_slice(own, add(own[:work], sent[0]), (0, 0))
        other = done[2][3]
        other = lax.dynamic_update_slice(other, add(other[work:], sent[1]), (work, 0))
        acc, other = sync(acc, other)
        acc, sent = shift(acc, nz), swap(other, "y")
        done = [done[i] for i in range(nz)]
        acts, d_gus, own, other = ([d[k] for d in done] for k in range(4))
        two_y, cot_y = [*both_y[:-1], both_y[-1][0]], [*both_y[:-1], both_y[-1][1]]
        lefts = [r for i in range(nz) for r in (both_z[i], two_y[i])]
        g_gu = shared_gradient(lefts, d_gus, 4, gw)
        g_gu, acc, sent = sync(g_gu, acc, sent)
        g_gu = lax.psum_scatter(g_gu, ("x", "c"), scatter_dimension=0, tiled=True)
        for i in range(2, nz):
            acc = sync(add(own[i], sent, acc))
            if i == nz - 1:
                break
            acc, sent = shift(acc, nz), swap(other[i + 1], "y")
            if i == 2:
                acc, sent, g_down = sync(acc, sent, down_gradient(acts, both_z, cot_y))
                g_down = lax.psum_scatter(g_down, ("x", "c"), scatter_dimension=0, tiled=True)
            else:
                acc, sent = sync(acc, sent)
        acc, sent = sync(shift(acc, nz), swap(other[0], "y"))
        total = own[0].astype(F32) + sent.astype(F32) + acc.astype(F32)
        d_hidden, d_gain_two = norm_back(total[:work], hidden, scale_two, gain_two)
        d_own = (grad_bf.astype(F32) + d_hidden).astype(BF16)
        delta = (attn + total[work:]).astype(BF16)
        d_hidden, d_own, delta, g_gu = sync(d_hidden, d_own, delta, g_gu)

        row_l, row_y = swap(d_own, "l"), swap(d_own, "y")
        slot_delta = rows_at(delta, row_of_slot)
        g_gu = lax.all_to_all(
            g_gu.reshape(nu, gw, -1), GROUP_F, split_axis=0, concat_axis=0, tiled=True
        )
        row_l, row_y, slot_delta = sync(row_l, row_y, slot_delta)
        row_ly = sync(swap(row_y[:half], "l"), swap(row_l[half:], "y"))
        g_qkv, mine, other, *part = attention_backward(
            (d_own, row_l, row_y, *row_ly),
            w_out,
            w_qkv,
            n_one,
            head_out,
            turned,
            cosine,
            sine,
            seg_col,
            seg_row,
            lax.axis_index("c").astype(jnp.int32).reshape(1),
            nt,
        )
        g_qkv, mine, other, part = sync(g_qkv, mine, other, part)
        g_qkv = lax.psum_scatter(
            g_qkv.reshape(width, -1), ("x", "c"), scatter_dimension=0, tiled=True
        )
        other = swap(other, "c")
        g_down, g_gu = sync(g_down, g_gu)

        def add_h(blocks):
            if nh != 2:
                return lax.psum_scatter(blocks, "h", scatter_dimension=0, tiled=False)
            mine, other = pick(blocks, "h")
            return add(mine, swap(other, "h"))

        def beside_last(pair_c):
            mine, other = pick(add(*pair_c), "x")
            return mine, swap(other, "x"), join_columns(g_gu), add_h(g_qkv.reshape(nh, nt * gw, -1))

        d_n_one, (mine, other, (g_gate, g_up), g_qkv) = sum_four(
            part, lambda: (mine, other), beside_last
        )
        d_norm, d_gain_one = norm_back(d_n_one, work_rows, scale_one, gain_one)
        back = (d_norm + d_hidden).astype(BF16)

        d_gains = jnp.concatenate([d_gain_one.reshape(n, gw), d_gain_two.reshape(n, gw)], axis=1)
        high = d_gains.astype(BF16)
        low = (d_gains - high.astype(F32)).astype(BF16)
        pad = jnp.zeros((n, cap - 2, 2 * gw), BF16)
        d_gains = jnp.concatenate([high[:, None], low[:, None], pad], axis=1)
        d_gains = jnp.pad(d_gains, ((0, 0), (0, 0), (0, extra - 2 * gw))).reshape(slots, extra)
        slot_back = rows_at(back, row_of_slot)
        slot_back = jnp.concatenate([slot_back, slot_delta, d_gains], axis=1)
        slot_back, g_qkv, mine, other = sync(slot_back, g_qkv, mine, other)
        got = to_all(slot_back)
        g_qkv = g_qkv.reshape(nt, gw, -1)
        g_out = add(mine, other)
        if nh == 2:
            g_out = pick(g_out, "h")
        else:
            g_out = (lax.psum_scatter(g_out, "h", scatter_dimension=0, tiled=False),)
        g_out = sync(g_out)
        own, to_l, to_y, to_ly = sync(
            *(lax.dynamic_index_in_dim(g_qkv, t_me ^ r, 0, False) for r in (0, 2, 1, 3))
        )
        to_l, to_y = swap(to_l, "l"), swap(to_y, "y")
        to_ly = lax.ppermute(to_ly, FOUR, [(i, 3 - i) for i in range(4)])
        g_out = tuple(lax.ppermute(p, ALL, to) for p, to in zip(g_out, (unperm, cross)))
        g_down = g_down.astype(F32)
        g_down, got = sync(g_down, got)
        d_gains = got[:, 2 * width :].reshape(n, cap, extra)[:, :2, : 2 * gw]
        d_gains = jnp.sum(d_gains.astype(F32), axis=(0, 1))
        local = rows_at(got, o.token)
        input_grad = (cotangent.astype(F32) + local[:, :width].astype(F32)).astype(BF16)
        output = (tokens.astype(F32) + local[:, width : 2 * width].astype(F32)).astype(BF16)
        own, to_l, to_y, to_ly, g_out, output, input_grad = sync(
            own, to_l, to_y, to_ly, g_out, output, input_grad
        )
        g_qkv = pair(pair(own, to_y, "y"), pair(to_l, to_ly, "y"), "l").reshape(nt, gw, -1)
        g_qkv = jnp.transpose(g_qkv.astype(F32), (1, 0, 2))
        g_out = sum(p.astype(F32) for p in g_out)
        g_query = g_qkv[:, :, :QW].reshape(gw, -1)
        g_key = g_qkv[:, :, QW : QW + HEAD_DIM].reshape(gw, -1)
        g_value = g_qkv[:, :, QW + HEAD_DIM :].reshape(gw, -1)
        return (
            output,
            input_grad,
            g_query,
            g_key,
            g_value,
            g_out,
            d_gains[:gw],
            g_gate,
            g_up,
            g_down,
            d_gains[gw:],
        )

    return shards


def solution(mesh):
    n = mesh.devices.size
    grid = Mesh(mesh.devices.reshape(n // 16, 2, 2, 2, 2), ALL)
    two, one = P(ALL, None), P(ALL)
    return jax.shard_map(
        make(n),
        mesh=grid,
        in_specs=(two, two, one, one, one, two, two, two, two, one, two, two, two, one),
        out_specs=(two, two, two, two, two, two, one, two, two, two, one),
        check_vma=False,
    )
```
